128 devices in a mesh: blk: 8 (over y, x_lo), grp: 16 (over x_hi, z, core).
Axes of the slice: x: 4 (x_hi: 2, x_lo: 2; x = x_hi * 2 + x_lo), y: 4, z: 4, core: 2. Of those that a mesh axis runs over, the one named last changes fastest.
Arguments:
- record: bfloat16 [16448, 32768], P(None, ('blk', 'grp')), may hold values from -400 to 400
- owner_order: int32 [4, 8], replicated, may hold values from 0 to 15, as said below
Outputs:
- cross_spectra: bfloat16 [4, 2, 16, 32768, 256], P(None, None, None, ('blk', 'grp'))
The draws below stay inside these ranges and needn't reach their ends.
Inputs may be any that keep to these rules, and one draw needn't show every extreme that they name: `owner_order`: a channel block position within a group.
All inputs are finite; a program needn't handle non-finite values.
Results may differ from the reference program's by a relative error of at most 0.0071.
Values may be sent and summed in bfloat16 or wider, within the bound.
A program may use at most 192 MiB of HBM per device.

```python
import math
import jax
import jax.numpy as jnp
from jax import lax

CH = 256
WIN = 256
NS = 128
NB = 16
BIN_LO = 8
ROUNDS = 4
HOP = 64
SAMPLES = 16448
GROUPS = 8
GROUP_BLOCKS = 16
CHANNELS = 32768
N_BLK = 8
N_GRP = 16


def draw_record(key, part):
    keys = jax.random.split(key, 3)
    chan_scale = jnp.exp(jax.random.uniform(keys[0], (CHANNELS,), jnp.float32, 0.0, math.log(10.0)))
    time_scale = jnp.exp(jax.random.uniform(keys[1], (WIN + 1,), jnp.float32, 0.0, math.log(10.0)))
    time_scale = jnp.repeat(time_scale, HOP)
    base = jnp.clip(jax.random.normal(keys[2], (SAMPLES, CHANNELS), jnp.float32), -4.0, 4.0)
    return (base * time_scale[:, None] * chan_scale[None, :]).astype(jnp.bfloat16)


def draw_owner_order(key, part):
    raw = jax.random.randint(key, (ROUNDS, GROUPS), 0, GROUP_BLOCKS, dtype=jnp.int32)
    chosen = jax.random.randint(jax.random.fold_in(key, 1), (), 0, GROUPS, dtype=jnp.int32)
    rows = jnp.arange(ROUNDS, dtype=jnp.int32)[:, None]
    cols = jnp.arange(GROUPS, dtype=jnp.int32)[None, :]
    raw = jnp.where((rows == 0) & (cols == chosen), GROUP_BLOCKS - 1, raw)
    raw = jnp.where((rows == 1) & (cols == chosen), 0, raw)
    return raw.astype(jnp.int32)


def setup_inputs(seed: int = 0) -> dict:
    key_of = jax.random.split(jax.random.key(seed), 3)
    return {
        "record": draw_record(jax.random.fold_in(key_of[2], 71), 0),
        "owner_order": draw_owner_order(jax.random.fold_in(key_of[2], 71), 0),
    }


def band_table():
    sample_index = jnp.arange(NS, dtype=jnp.int32)
    bin_index = BIN_LO + jnp.arange(NB, dtype=jnp.int32)
    phase_int = bin_index[:, None] * sample_index[None, :] % NS
    phase = phase_int.astype(jnp.float32) * (2.0 * math.pi / NS)
    taper = 0.5 - 0.5 * jnp.cos(sample_index.astype(jnp.float32) * (2.0 * math.pi / NS))
    scale = 1.0 / math.sqrt(3.0 * NS / 8.0)
    real_rows = taper[None, :] * jnp.cos(phase) * scale
    imag_rows = -taper[None, :] * jnp.sin(phase) * scale
    return jnp.concatenate([real_rows, imag_rows], axis=0).astype(jnp.bfloat16)

def block_spectra(samples, table):
    halves = samples.reshape(WIN + 1, HOP, samples.shape[1]).astype(jnp.float32)
    table_wide = table.astype(jnp.float32)
    first_half = jnp.einsum('kn,hnc->hkc', table_wide[:, :HOP], halves)
    second_half = jnp.einsum('kn,hnc->hkc', table_wide[:, HOP:], halves)
    half_energy = lax.optimization_barrier(jnp.sum(halves * halves, axis=1))
    window_rms = jnp.sqrt((half_energy[:-1] + half_energy[1:]) / NS + 1e-05)
    raw = first_half[:-1] + second_half[1:]
    return (raw / window_rms[:, None, :]).astype(jnp.bfloat16)

def cross_stack(own, other):
    own_wide = own.astype(jnp.float32)
    other_wide = other.astype(jnp.float32)
    real_own, imag_own = (own_wide[:, :NB], own_wide[:, NB:])
    real_other, imag_other = (other_wide[:, :NB], other_wide[:, NB:])
    real_part = jnp.einsum('wfi,wfj->fij', real_own, real_other) + jnp.einsum('wfi,wfj->fij', imag_own, imag_other)
    imag_part = jnp.einsum('wfi,wfj->fij', imag_own, real_other) - jnp.einsum('wfi,wfj->fij', real_own, imag_other)
    return jnp.stack([real_part, imag_part], axis=0) / math.sqrt(WIN)

def reference(record, owner_order):
    table = band_table()
    blocks = N_BLK * N_GRP

    def one_block(index):
        samples = lax.dynamic_slice_in_dim(record, (index * CH).astype(jnp.int32), CH, 1)
        return block_spectra(samples, table)
    all_spectra = lax.map(one_block, jnp.arange(blocks, dtype=jnp.int32))

    def one_pair_set(index):
        my_group = index // N_GRP
        results = []
        for round_index in range(ROUNDS):
            partner = (my_group - round_index) % N_BLK * N_GRP + owner_order[round_index, my_group]
            results.append(cross_stack(all_spectra[index], all_spectra[partner.astype(jnp.int32)]))
        return jnp.stack(results, axis=0).astype(jnp.bfloat16)
    stacked = lax.map(one_pair_set, jnp.arange(blocks, dtype=jnp.int32))
    stacked = jnp.transpose(stacked, (1, 2, 3, 0, 4, 5))
    return stacked.reshape(ROUNDS, 2, NB, blocks * CH, CH)
```

```python
import functools
import math

import jax
import jax.numpy as jnp
import numpy as np
from jax import lax
from jax.experimental import pallas as pl
from jax.experimental.pallas import tpu as pltpu
from jax.sharding import PartitionSpec as P

WIN = 256
NS = 128
NB = 16
BIN_LO = 8
ROUNDS = 4
HOP = 64
CH = 256
GW = 8
STEPW = 32
NCH = 2
PIECE = 1024
ROWS = PIECE // NCH
MESH = pl.DeviceIdType.MESH


def band_table():
    sample_index = np.arange(NS, dtype=np.int64)
    bin_index = BIN_LO + np.arange(NB, dtype=np.int64)
    phase = (bin_index[:, None] * sample_index[None, :] % NS) * (2.0 * math.pi / NS)
    taper = 0.5 - 0.5 * np.cos(sample_index * (2.0 * math.pi / NS))
    scale = 1.0 / math.sqrt(3.0 * NS / 8.0)
    real_rows = taper[None, :] * np.cos(phase) * scale
    imag_rows = -taper[None, :] * np.sin(phase) * scale
    return np.stack([real_rows, imag_rows], axis=1).reshape(2 * NB, NS)


def banded_table():
    table = band_table()
    wide = np.zeros((2 * NB, GW, HOP * (GW + 1)), np.float32)
    for w in range(GW):
        wide[:, w, w * HOP : w * HOP + NS] = table
    return wide.reshape(2 * NB * GW, HOP * (GW + 1)).astype(jnp.bfloat16)


def spectra_kernel(t_ref, main_ref, tail_ref, o_ref):
    parts = []
    for s in range(STEPW // GW):
        lo = s * GW * HOP
        if s < STEPW // GW - 1:
            x = main_ref[lo : lo + (GW + 1) * HOP, :]
        else:
            x = jnp.concatenate([main_ref[lo : lo + GW * HOP, :], tail_ref[...]], axis=0)
        raw = jnp.dot(t_ref[...], x, preferred_element_type=jnp.float32)
        wide = x.astype(jnp.float32)
        energy = jnp.sum((wide * wide).reshape(GW + 1, HOP, CH), axis=1)
        inv = 1.0 / jnp.sqrt((energy[:GW] + energy[1:]) / NS + 1e-05)
        parts.append(raw.reshape(2 * NB, GW, CH) * inv[None])
        if s % 2 == 1:
            both = jnp.concatenate(parts, axis=1).astype(jnp.bfloat16)
            o_ref[:, (s - 1) * GW : (s + 1) * GW, :] = both
            parts = []


def spectra(record):
    steps = WIN // STEPW
    return pl.pallas_call(
        spectra_kernel,
        grid=(steps,),
        out_shape=jax.ShapeDtypeStruct((2 * NB, WIN, CH), jnp.bfloat16),
        in_specs=[
            pl.BlockSpec((2 * NB * GW, HOP * (GW + 1)), lambda g: (0, 0)),
            pl.BlockSpec((STEPW * HOP, CH), lambda g: (g, 0)),
            pl.BlockSpec((HOP, CH), lambda g: ((g + 1) * STEPW, 0)),
        ],
        out_specs=pl.BlockSpec((2 * NB, STEPW, CH), lambda g: (0, g, 0)),
        compiler_params=pltpu.CompilerParams(vmem_limit_bytes=48 * 2**20),
        name="spectra",
    )(jnp.asarray(banded_table()), record, record)


NSEM = 48


def exchange_kernel(order_ref, s_ref, g_ref, *scratch):
    it = iter(scratch)
    a_buf = [next(it) for _ in range(NCH)]
    b_send = [[next(it) for _ in range(2)] for _ in range(NCH)]
    b_recv = [[next(it) for _ in range(ROUNDS)] for _ in range(NCH)]
    merged = [[next(it) for _ in range(ROUNDS)] for _ in range(NCH)]
    final = [[next(it) for _ in range(ROUNDS)] for _ in range(NCH)]
    hop1 = [next(it) for _ in range(NCH)]
    ssem, rsem, lsem = next(it), next(it), next(it)

    blk = lax.axis_index("blk")
    grp = lax.axis_index("grp")
    y, par = blk // 2, blk % 2
    xhi, z, core = grp // 8, (grp // 2) % 4, grp % 2

    def chip(dx, dy, dz, other):
        x = (xhi * 2 + par + dx + 4) % 4
        yy = (y + dy + 4) % 4
        zz = (z + dz + 4) % 4
        c = 1 - core if other else core
        return (yy * 2 + x % 2, (x // 2) * 8 + zz * 2 + c)

    def rows(j):
        return pl.ds(j * ROWS, ROWS)

    counters = [[0] for _ in range(NCH)]

    def remote(j, src, dst, device):
        k = counters[j][0]
        counters[j][0] += 1
        cp = pltpu.make_async_remote_copy(
            src_ref=src, dst_ref=dst, send_sem=ssem.at[j, k], recv_sem=rsem.at[j, k],
            device_id=device, device_id_type=MESH,
        )
        cp.start()
        return cp

    def copy_rows(dst, load):
        step = 64

        def run(i, carry):
            at = pl.ds(i * step, step)
            dst[at, :] = load(at)
            return carry

        lax.fori_loop(0, ROWS // step, run, 0)

    sent = []

    a_copies = [[] for _ in range(NCH)]
    slot = z * 2 + core

    def start_a(j):
        for dz, other in ((2, 0), (2, 1), (1, 0), (3, 0), (1, 1), (3, 1), (0, 1)):
            zz = (z + dz) % 4
            c = 1 - core if other else core
            a_copies[j].append(
                remote(j, s_ref.at[zz * 2 + c, rows(j)], a_buf[j].at[slot], chip(0, 0, dz, other))
            )
        own = pltpu.make_async_copy(s_ref.at[slot, rows(j)], a_buf[j].at[slot], lsem.at[j, 0])
        own.start()
        return own

    owns = {}
    b_copies = [[[] for _ in range(ROUNDS)] for _ in range(NCH)]
    h_copies = [[None] * ROUNDS for _ in range(NCH)]
    c_copies = [[None] * ROUNDS for _ in range(NCH)]
    locals_ = []

    def pick_and_send(j):
        owns[j].wait()
        for cp in a_copies[j]:
            cp.wait_recv()
        for r in range(ROUNDS):
            owner = order_ref[r, (blk + r) % 8] % 8
            if r % 2 == 0:
                dst = b_recv[j][r].at[xhi]
            else:
                dst = b_send[j][r // 2]
            copy_rows(dst, lambda at: a_buf[j][owner, at, :])
            for dx in ((2,) if r % 2 == 0 else (1, -1)):
                b_copies[j][r].append(remote(j, dst, b_recv[j][r].at[xhi], chip(dx, 0, 0, 0)))

    def merge_and_hop(j):
        for r in range(ROUNDS):
            for cp in b_copies[j][r]:
                cp.wait_recv()
            source = blk if r % 2 == 0 else blk + 1 - 2 * par
            column = order_ref[r, (source + r) % 8] // 8
            dst = final[j][r] if r == 0 else merged[j][r]
            copy_rows(dst, lambda at: b_recv[j][r][column, at, :])
            if r == 0:
                gather(j, r)
            else:
                dy = 2 - par if r == 3 else 1
                land = hop1[j] if r == 1 else final[j][r]
                h_copies[j][r] = remote(j, dst, land, chip(0, dy, 0, 0))

    def hopped(j):
        for r in range(1, ROUNDS):
            h_copies[j][r].wait_recv()
            if r == 1:
                copy_rows(
                    final[j][r],
                    lambda at: jnp.where(par == 0, hop1[j][at, :], merged[j][r][at, :]),
                )
            gather(j, r)

    def place(r, zz, c, j):
        return g_ref.at[r, zz * 2 + c, rows(j)]

    def half(r, zz, c, j, h):
        return g_ref.at[r, zz * 2 + c, pl.ds(j * ROWS + h * (ROWS // 2), ROWS // 2)]

    def gather(j, r):
        up = remote(j, final[j][r], place(r, z, core, j), chip(0, 0, 1, 0))
        down = remote(j, final[j][r], place(r, z, core, j), chip(0, 0, -1, 0))
        side = remote(j, final[j][r], place(r, z, core, j), chip(0, 0, 0, 1))
        own = pltpu.make_async_copy(final[j][r], place(r, z, core, j), lsem.at[j, 1 + r])
        own.start()
        locals_.append(own)
        c_copies[j][r] = [up, down, side]

    def forward(j, r):
        up, down, side = c_copies[j][r]
        below, above = (z + 3) % 4, (z + 1) % 4
        up.wait_recv()
        f_up = remote(j, half(r, below, core, j, 0), half(r, below, core, j, 0), chip(0, 0, 1, 0))
        s_below = remote(j, place(r, below, core, j), place(r, below, core, j), chip(0, 0, 0, 1))
        down.wait_recv()
        f_down = remote(j, half(r, above, core, j, 1), half(r, above, core, j, 1), chip(0, 0, -1, 0))
        s_above = remote(j, place(r, above, core, j), place(r, above, core, j), chip(0, 0, 0, 1))
        c_copies[j][r] += [f_up, f_down, s_below, s_above]

    def finish(j, r):
        up, down, side, f_up, f_down, s_below, s_above = c_copies[j][r]
        f_up.wait_recv()
        f_down.wait_recv()
        far = (z + 2) % 4
        s_far = remote(j, place(r, far, core, j), place(r, far, core, j), chip(0, 0, 0, 1))
        for cp in (side, s_below, s_above, s_far):
            sent.append(cp)
        c_copies[j][r].append(s_far)

    owns[0] = start_a(0)
    if NCH > 1:
        owns[1] = start_a(1)
    stages = NCH + 4
    for t in range(stages):
        if t < NCH:
            pick_and_send(t)
            if t + 2 < NCH:
                owns[t + 2] = start_a(t + 2)
        if 0 <= t - 1 < NCH:
            merge_and_hop(t - 1)
        if 0 <= t - 2 < NCH:
            forward(t - 2, 0)
            hopped(t - 2)
        if 0 <= t - 3 < NCH:
            for r in range(1, ROUNDS):
                forward(t - 3, r)
            finish(t - 3, 0)
        if 0 <= t - 4 < NCH:
            for r in range(1, ROUNDS):
                finish(t - 4, r)
    for cp in sent:
        cp.wait_recv()
    for cp in locals_:
        cp.wait()
    for j in range(NCH):
        for cp in a_copies[j]:
            cp.wait_send()
        for r in range(ROUNDS):
            for cp in b_copies[j][r]:
                cp.wait_send()
            if h_copies[j][r] is not None:
                h_copies[j][r].wait_send()
            for cp in c_copies[j][r]:
                cp.wait_send()


def exchange(order, s):
    bf16 = jnp.bfloat16
    buf = lambda *lead: pltpu.VMEM(lead + (ROWS, CH), bf16)
    scratch = [buf(8) for _ in range(NCH)]
    scratch += [buf() for _ in range(2 * NCH)]
    scratch += [buf(2) for _ in range(ROUNDS * NCH)]
    scratch += [buf() for _ in range(ROUNDS * NCH)]
    scratch += [buf() for _ in range(ROUNDS * NCH)]
    scratch += [buf() for _ in range(NCH)]
    scratch += [
        pltpu.SemaphoreType.DMA((NCH, NSEM)),
        pltpu.SemaphoreType.DMA((NCH, NSEM)),
        pltpu.SemaphoreType.DMA((NCH, 1 + ROUNDS)),
    ]
    return pl.pallas_call(
        exchange_kernel,
        out_shape=jax.ShapeDtypeStruct((ROUNDS, 8, PIECE, CH), bf16),
        in_specs=[
            pl.BlockSpec(memory_space=pltpu.SMEM),
            pl.BlockSpec(memory_space=pl.ANY),
        ],
        out_specs=pl.BlockSpec(memory_space=pl.ANY),
        scratch_shapes=scratch,
        compiler_params=pltpu.CompilerParams(
            has_side_effects=True, vmem_limit_bytes=56 * 2**20
        ),
        name="exchange",
    )(order, s.reshape(8, PIECE, CH))


def cross_kernel(own_ref, other_ref, o_ref):
    x = own_ref[0]
    p, q = x[:WIN].astype(jnp.float32), x[WIN:].astype(jnp.float32)
    scale = 1.0 / math.sqrt(WIN)
    pt = (p.T * scale).astype(jnp.bfloat16)
    qt = (q.T * scale).astype(jnp.bfloat16)
    left = jnp.concatenate(
        [jnp.concatenate([pt, qt], axis=1), jnp.concatenate([qt, -pt], axis=1)], axis=0
    )
    for r in range(ROUNDS):
        out = jnp.dot(left, other_ref[r, 0], preferred_element_type=jnp.float32)
        o_ref[r, 0, 0] = out[:CH].astype(jnp.bfloat16)
        o_ref[r, 1, 0] = out[CH:].astype(jnp.bfloat16)


def cross(s, g):
    return pl.pallas_call(
        cross_kernel,
        grid=(NB,),
        out_shape=jax.ShapeDtypeStruct((ROUNDS, 2, NB, CH, CH), jnp.bfloat16),
        in_specs=[
            pl.BlockSpec((1, 2 * WIN, CH), lambda f: (f, 0, 0)),
            pl.BlockSpec((ROUNDS, 1, 2 * WIN, CH), lambda f: (0, f, 0, 0)),
        ],
        out_specs=pl.BlockSpec((ROUNDS, 2, 1, CH, CH), lambda f: (0, 0, f, 0, 0)),
        compiler_params=pltpu.CompilerParams(vmem_limit_bytes=48 * 2**20),
        name="cross",
    )(s.reshape(NB, 2 * WIN, CH), g.reshape(ROUNDS, NB, 2 * WIN, CH))


def body(record, owner_order):
    s = spectra(record)
    g = exchange(owner_order, s)
    return cross(s, g)


def solution(mesh):
    placed = (P(None, ("blk", "grp")), P())
    return jax.shard_map(
        body,
        mesh=mesh,
        in_specs=placed,
        out_specs=P(None, None, None, ("blk", "grp"), None),
        check_vma=False,
    )
```

```python
import functools
import math

import jax
import jax.numpy as jnp
import numpy as np
from jax import lax
from jax.experimental import pallas as pl
from jax.experimental.pallas import tpu as pltpu
from jax.sharding import PartitionSpec as P

WIN = 256
NS = 128
NB = 16
BIN_LO = 8
ROUNDS = 4
HOP = 64
CH = 256
GW = 8
STEPW = 16
PIECE = 1024
PLAN = ((2, True), (2, False)) * 4
AHEAD = 2
AGES = (0, 2, 4, 6, 8)
MESH = pl.DeviceIdType.MESH


def band_table():
    sample_index = np.arange(NS, dtype=np.int64)
    bin_index = BIN_LO + np.arange(NB, dtype=np.int64)
    phase = (bin_index[:, None] * sample_index[None, :] % NS) * (2.0 * math.pi / NS)
    taper = 0.5 - 0.5 * np.cos(sample_index * (2.0 * math.pi / NS))
    scale = 1.0 / math.sqrt(3.0 * NS / 8.0)
    real_rows = taper[None, :] * np.cos(phase) * scale
    imag_rows = -taper[None, :] * np.sin(phase) * scale
    return np.stack([real_rows, imag_rows], axis=1).reshape(2 * NB, NS)


def banded_table():
    table = band_table()
    wide = np.zeros((2 * NB, GW, HOP * (GW + 1)), np.float32)
    for w in range(GW):
        wide[:, w, w * HOP : w * HOP + NS] = table
    return wide.reshape(2 * NB * GW, HOP * (GW + 1)).astype(jnp.bfloat16)


def spectra_kernel(t_ref, main_ref, tail_ref, o_ref):
    parts = []
    for s in range(STEPW // GW):
        lo = s * GW * HOP
        if s < STEPW // GW - 1:
            x = main_ref[lo : lo + (GW + 1) * HOP, :]
        else:
            x = jnp.concatenate([main_ref[lo : lo + GW * HOP, :], tail_ref[...]], axis=0)
        raw = jnp.dot(t_ref[...], x, preferred_element_type=jnp.float32)
        wide = x.astype(jnp.float32)
        energy = jnp.sum((wide * wide).reshape(GW + 1, HOP, CH), axis=1)
        inv = 1.0 / jnp.sqrt((energy[:GW] + energy[1:]) / NS + 1e-05)
        parts.append(raw.reshape(2 * NB, GW, CH) * inv[None])
        if s % 2 == 1:
            both = jnp.concatenate(parts, axis=1).astype(jnp.bfloat16)
            o_ref[:, 0, :, (s - 1) * GW : (s + 1) * GW, :] = both.reshape(8, 4, 2 * GW, CH)
            parts = []


def spectra(record):
    steps = WIN // STEPW
    out = pl.pallas_call(
        spectra_kernel,
        grid=(steps,),
        out_shape=jax.ShapeDtypeStruct((8, steps, 4, STEPW, CH), jnp.bfloat16),
        in_specs=[
            pl.BlockSpec((2 * NB * GW, HOP * (GW + 1)), lambda g: (0, 0)),
            pl.BlockSpec((STEPW * HOP, CH), lambda g: (g, 0)),
            pl.BlockSpec((HOP, CH), lambda g: ((g + 1) * STEPW, 0)),
        ],
        out_specs=pl.BlockSpec((8, 1, 4, STEPW, CH), lambda g: (0, g, 0, 0, 0)),
        compiler_params=pltpu.CompilerParams(vmem_limit_bytes=48 * 2**20),
        name="spectra",
    )(jnp.asarray(banded_table()), record, record)
    return out.reshape(8, PIECE, CH)


NSEM = 32
WB_ROWS = 4 * STEPW
CHUNKS = []
for blocks, shared in PLAN:
    first = CHUNKS[-1][0] + CHUNKS[-1][1] if CHUNKS else 0
    CHUNKS.append((first, blocks * WB_ROWS, shared))
NCH = len(CHUNKS)


def exchange_kernel(order_ref, s_ref, g_ref, *scratch):
    it = iter(scratch)
    a_buf = [next(it) for _ in range(NCH)]
    b_send = [next(it) for _ in range(NCH)]
    b_recv = [next(it) for _ in range(NCH)]
    final = [next(it) for _ in range(NCH)]
    ssem, rsem, lsem = next(it), next(it), next(it)

    blk = lax.axis_index("blk")
    grp = lax.axis_index("grp")
    y, par = blk // 2, blk % 2
    xhi, z, core = grp // 8, (grp // 2) % 4, grp % 2
    slot = z * 2 + core
    below, above, far = (z + 3) % 4, (z + 1) % 4, (z + 2) % 4

    def device(dx, dy, dz, other):
        x = (xhi * 2 + par + dx + 4) % 4
        yy = (y + dy + 4) % 4
        zz = (z + dz + 4) % 4
        c = 1 - core if other else core
        return (yy * 2 + x % 2, (x // 2) * 8 + zz * 2 + c)

    counters = [0] * NCH
    everything = []

    def remote(j, src, dst, target):
        k = counters[j]
        counters[j] += 1
        cp = pltpu.make_async_remote_copy(
            src_ref=src, dst_ref=dst, send_sem=ssem.at[j, k], recv_sem=rsem.at[j, k],
            device_id=target, device_id_type=MESH,
        )
        cp.start()
        everything.append(cp)
        return cp

    def copy_rows(count, store, load):
        step = 32

        def run(i, carry):
            at = pl.multiple_of(i * step, step)
            store(at, step, load(at, step))
            return carry

        lax.fori_loop(0, count // step, run, 0)

    def width(j):
        return CHUNKS[j][1] // 2

    def place(zz, j, column, part=None):
        w = width(j)
        lo = CHUNKS[j][0] + column * w
        if part is not None and CHUNKS[j][2]:
            w = w // 2
            lo = lo + part * w
        elif part is not None:
            lo = CHUNKS[j][0] + part * w
        return g_ref.at[:, zz * 2 + core, pl.ds(pl.multiple_of(lo, 16), w)]

    def gathered(zz, j):
        if CHUNKS[j][2]:
            return place(zz, j, xhi)
        return g_ref.at[:, zz * 2 + core, pl.ds(CHUNKS[j][0], CHUNKS[j][1])]

    a_copies = [[] for _ in range(NCH)]
    locals_ = [[] for _ in range(NCH)]

    def start_a(j):
        rows = pl.ds(CHUNKS[j][0], CHUNKS[j][1])
        for dz, other in ((2, 0), (2, 1), (1, 0), (3, 0), (1, 1), (3, 1), (0, 1)):
            zz = (z + dz) % 4
            c = 1 - core if other else core
            a_copies[j].append(
                remote(j, s_ref.at[zz * 2 + c, rows], a_buf[j].at[slot], device(0, 0, dz, other))
            )
        own = pltpu.make_async_copy(s_ref.at[slot, rows], a_buf[j].at[slot], lsem.at[j, 0])
        own.start()
        locals_[j].append(own)

    b_copies = [[] for _ in range(NCH)]

    def pick_and_send(j):
        locals_[j][0].wait()
        for cp in a_copies[j]:
            cp.wait_recv()
        w = width(j)
        for r in range(ROUNDS):
            owner = order_ref[r, (blk + r) % 8] % 8

            if r == 0:
                base = pl.multiple_of(xhi * w, 16)

                def keep(at, n, value):
                    b_recv[j][0, xhi, pl.ds(at, n), :] = value

                copy_rows(w, keep, lambda at, n: a_buf[j][owner, pl.ds(base + at, n), :])

            def store(at, n, value):
                b_send[j][r, pl.ds(at, n), :] = value

            copy_rows(CHUNKS[j][1], store, lambda at, n: a_buf[j][owner, pl.ds(at, n), :])
            moves = (
                ((2, 0),),
                ((1, par), (-1, par)),
                ((0, 1), (2, 1)),
                ((1, 1 + par), (-1, 1 + par)),
            )[r]
            for dx, dy in moves:
                column = ((xhi * 2 + par + dx + 4) % 4) // 2
                src = b_send[j].at[r, pl.ds(pl.multiple_of(column * w, 16), w)]
                b_copies[j].append(
                    remote(j, src, b_recv[j].at[r, xhi], device(dx, dy, 0, 0))
                )

    c_copies = [None] * NCH
    x_copies = [[] for _ in range(NCH)]
    sides = []

    def spread(j, zz, src):
        sides.append(remote(j, src, gathered(zz, j), device(0, 0, 0, 1)))
        if CHUNKS[j][2]:
            x_copies[j].append((zz, remote(j, src, place(zz, j, xhi), device(2, 0, 0, 0))))

    def merge(j):
        for cp in b_copies[j]:
            cp.wait_recv()
        for r in range(ROUNDS):
            column = order_ref[r, blk] // 8

            def store(at, n, value):
                final[j][r, pl.ds(at, n), :] = value

            copy_rows(width(j), store, lambda at, n: b_recv[j][r, column, pl.ds(at, n), :])
        own = pltpu.make_async_copy(final[j], place(z, j, xhi), lsem.at[j, 1])
        own.start()
        locals_[j].append(own)
        if CHUNKS[j][2]:
            gather(j, final[j])
        else:
            x_copies[j].append((z, remote(j, final[j], place(z, j, xhi), device(2, 0, 0, 0))))

    def gather(j, src):
        up = remote(j, src, gathered(z, j), device(0, 0, 1, 0))
        down = remote(j, src, gathered(z, j), device(0, 0, -1, 0))
        spread(j, z, src)
        c_copies[j] = [up, down]

    def complete(j):
        x_copies[j][0][1].wait_recv()
        locals_[j][1].wait()
        gather(j, gathered(z, j))

    def forward(j):
        up, down = c_copies[j]
        up.wait_recv()
        part = place(below, j, xhi, 0)
        f_up = remote(j, part, part, device(0, 0, 1, 0))
        spread(j, below, gathered(below, j))
        down.wait_recv()
        part = place(above, j, xhi, 1)
        f_down = remote(j, part, part, device(0, 0, -1, 0))
        spread(j, above, gathered(above, j))
        c_copies[j] = [f_up, f_down]

    def forwarded(j):
        for cp in c_copies[j]:
            cp.wait_recv()
        spread(j, far, gathered(far, j))

    def crossed(j):
        for zz, cp in x_copies[j]:
            cp.wait_recv()
            part = place(zz, j, 1 - xhi)
            sides.append(remote(j, part, part, device(0, 0, 0, 1)))

    steps = {
        True: (pick_and_send, merge, forward, forwarded, crossed),
        False: (pick_and_send, merge, complete, forward, forwarded),
    }
    for j in range(AHEAD):
        start_a(j)
    for t in range(NCH + max(AGES)):
        for stage in (4, 3, 2, 1, 0):
            j = t - AGES[stage]
            if 0 <= j < NCH:
                steps[CHUNKS[j][2]][stage](j)
                if stage == 0 and j + AHEAD < NCH:
                    start_a(j + AHEAD)
    for cp in sides:
        cp.wait_recv()
    for j in range(NCH):
        if CHUNKS[j][2]:
            locals_[j][1].wait()
    for cp in everything:
        cp.wait_send()


def exchange(order, s):
    bf16 = jnp.bfloat16
    sizes = [(n, n // 2) for _, n, _ in CHUNKS]
    scratch = [pltpu.VMEM((8, n, CH), bf16) for n, _ in sizes]
    scratch += [pltpu.VMEM((ROUNDS, n, CH), bf16) for n, _ in sizes]
    scratch += [pltpu.VMEM((ROUNDS, 2, w, CH), bf16) for _, w in sizes]
    scratch += [pltpu.VMEM((ROUNDS, w, CH), bf16) for _, w in sizes]
    scratch += [
        pltpu.SemaphoreType.DMA((NCH, NSEM)),
        pltpu.SemaphoreType.DMA((NCH, NSEM)),
        pltpu.SemaphoreType.DMA((NCH, 2)),
    ]
    return pl.pallas_call(
        exchange_kernel,
        out_shape=jax.ShapeDtypeStruct((ROUNDS, 8, PIECE, CH), bf16),
        in_specs=[
            pl.BlockSpec(memory_space=pltpu.SMEM),
            pl.BlockSpec(memory_space=pl.ANY),
        ],
        out_specs=pl.BlockSpec(memory_space=pl.ANY),
        scratch_shapes=scratch,
        compiler_params=pltpu.CompilerParams(
            has_side_effects=True, vmem_limit_bytes=56 * 2**20
        ),
        name="exchange",
    )(order, s)


def cross_kernel(own_ref, other_ref, o_ref):
    own = own_ref[0].reshape(WIN // STEPW, 4, STEPW, CH)
    for b in range(2):
        p = own[:, 2 * b].reshape(WIN, CH)
        q = own[:, 2 * b + 1].reshape(WIN, CH)
        pt, qt = p.T, q.T
        left = jnp.concatenate(
            [jnp.concatenate([pt, qt], axis=1), jnp.concatenate([qt, -pt], axis=1)], axis=0
        )
        for r in range(ROUNDS):
            other = other_ref[r, 0].reshape(WIN // STEPW, 4, STEPW, CH)
            right = jnp.concatenate(
                [other[:, 2 * b].reshape(WIN, CH), other[:, 2 * b + 1].reshape(WIN, CH)], axis=0
            )
            out = jnp.dot(left, right, preferred_element_type=jnp.float32)
            out = (out * (1.0 / math.sqrt(WIN))).astype(jnp.bfloat16)
            o_ref[r, 0, b] = out[:CH]
            o_ref[r, 1, b] = out[CH:]


def cross(s, g):
    return pl.pallas_call(
        cross_kernel,
        grid=(8,),
        out_shape=jax.ShapeDtypeStruct((ROUNDS, 2, NB, CH, CH), jnp.bfloat16),
        in_specs=[
            pl.BlockSpec((1, PIECE, CH), lambda f: (f, 0, 0)),
            pl.BlockSpec((ROUNDS, 1, PIECE, CH), lambda f: (0, f, 0, 0)),
        ],
        out_specs=pl.BlockSpec((ROUNDS, 2, 2, CH, CH), lambda f: (0, 0, f, 0, 0)),
        compiler_params=pltpu.CompilerParams(vmem_limit_bytes=48 * 2**20),
        name="cross",
    )(s, g)


def body(record, owner_order):
    s = spectra(record)
    g = exchange(owner_order, s)
    return cross(s, g)


def solution(mesh):
    placed = (P(None, ("blk", "grp")), P())
    return jax.shard_map(
        body,
        mesh=mesh,
        in_specs=placed,
        out_specs=P(None, None, None, ("blk", "grp"), None),
        check_vma=False,
    )
```

```python
import functools
import math

import jax
import jax.numpy as jnp
import numpy as np
from jax import lax
from jax.experimental import pallas as pl
from jax.experimental.pallas import tpu as pltpu
from jax.sharding import PartitionSpec as P

WIN = 256
NS = 128
NB = 16
BIN_LO = 8
ROUNDS = 4
HOP = 64
CH = 256
GW = 8
STEPW = 16
PIECE = 1024
PLAN = ((2, True), (2, False)) * 4
AHEAD = 2
AGES = (0, 2, 4, 6, 8)
MESH = pl.DeviceIdType.MESH


def band_table():
    sample_index = np.arange(NS, dtype=np.int64)
    bin_index = BIN_LO + np.arange(NB, dtype=np.int64)
    phase = (bin_index[:, None] * sample_index[None, :] % NS) * (2.0 * math.pi / NS)
    taper = 0.5 - 0.5 * np.cos(sample_index * (2.0 * math.pi / NS))
    scale = 1.0 / math.sqrt(3.0 * NS / 8.0)
    real_rows = taper[None, :] * np.cos(phase) * scale
    imag_rows = -taper[None, :] * np.sin(phase) * scale
    return np.stack([real_rows, imag_rows], axis=1).reshape(2 * NB, NS)


def banded_table():
    table = band_table()
    wide = np.zeros((2 * NB, GW, HOP * (GW + 1)), np.float32)
    for w in range(GW):
        wide[:, w, w * HOP : w * HOP + NS] = table
    return wide.reshape(2 * NB * GW, HOP * (GW + 1)).astype(jnp.bfloat16)


NSEM = 32
WB_ROWS = 4 * STEPW
CHUNKS = []
for blocks, shared in PLAN:
    first = CHUNKS[-1][0] + CHUNKS[-1][1] if CHUNKS else 0
    CHUNKS.append((first, blocks * WB_ROWS, shared))
NCH = len(CHUNKS)


def exchange_kernel(order_in, t_in, rec_ref, g_ref, own_ref, *scratch):
    it = iter(scratch)
    order_ref, t_ref = next(it), next(it)
    rec, s_ref = next(it), next(it)
    a_buf = [next(it) for _ in range(NCH)]
    b_send = [next(it) for _ in range(NCH)]
    b_recv = [next(it) for _ in range(NCH)]
    final = [next(it) for _ in range(NCH)]
    ssem, rsem, lsem, isem = next(it), next(it), next(it), next(it)

    blk = lax.axis_index("blk")
    grp = lax.axis_index("grp")
    y, par = blk // 2, blk % 2
    xhi, z, core = grp // 8, (grp // 2) % 4, grp % 2
    slot = z * 2 + core
    below, above, far = (z + 3) % 4, (z + 1) % 4, (z + 2) % 4

    def device(dx, dy, dz, other):
        x = (xhi * 2 + par + dx + 4) % 4
        yy = (y + dy + 4) % 4
        zz = (z + dz + 4) % 4
        c = 1 - core if other else core
        return (yy * 2 + x % 2, (x // 2) * 8 + zz * 2 + c)

    counters = [0] * NCH
    everything = []

    def remote(j, src, dst, target):
        k = counters[j]
        counters[j] += 1
        cp = pltpu.make_async_remote_copy(
            src_ref=src, dst_ref=dst, send_sem=ssem.at[j, k], recv_sem=rsem.at[j, k],
            device_id=target, device_id_type=MESH,
        )
        cp.start()
        everything.append(cp)
        return cp

    def copy_rows(count, store, load):
        step = 32

        def run(i, carry):
            at = pl.multiple_of(i * step, step)
            store(at, step, load(at, step))
            return carry

        lax.fori_loop(0, count // step, run, 0)

    def width(j):
        return CHUNKS[j][1] // 2

    def place(zz, j, column, part=None):
        w = width(j)
        lo = CHUNKS[j][0] + column * w
        if part is not None and CHUNKS[j][2]:
            w = w // 2
            lo = lo + part * w
        elif part is not None:
            lo = CHUNKS[j][0] + part * w
        return g_ref.at[:, zz * 2 + core, pl.ds(pl.multiple_of(lo, 16), w)]

    def gathered(zz, j):
        if CHUNKS[j][2]:
            return place(zz, j, xhi)
        return g_ref.at[:, zz * 2 + core, pl.ds(CHUNKS[j][0], CHUNKS[j][1])]

    small = [
        pltpu.make_async_copy(t_in, t_ref, isem.at[2 * NCH]),
        pltpu.make_async_copy(order_in, order_ref, isem.at[2 * NCH + 1]),
    ]
    small[0].start()
    reads = []
    for j in range(NCH):
        lo = CHUNKS[j][0] // 4 * HOP + (HOP if j else 0)
        hi = (CHUNKS[j][0] + CHUNKS[j][1]) // 4 * HOP + HOP
        rows = pl.ds(lo, hi - lo)
        reads.append(pltpu.make_async_copy(rec_ref.at[rows], rec.at[rows], isem.at[j]))
        reads[j].start()

    small[1].start()

    def compute(j):
        if j == 0:
            small[0].wait()
            small[1].wait()
        reads[j].wait()
        first = CHUNKS[j][0] // WB_ROWS

        def run(i, carry):
            block = first + i
            parts = []
            for half in range(STEPW // GW):
                at = pl.multiple_of(block * (STEPW * HOP) + half * (GW * HOP), HOP)
                x = rec[pl.ds(at, (GW + 1) * HOP), :]
                raw = jnp.dot(t_ref[...], x, preferred_element_type=jnp.float32)
                wide = x.astype(jnp.float32)
                energy = jnp.sum((wide * wide).reshape(GW + 1, HOP, CH), axis=1)
                inv = 1.0 / jnp.sqrt((energy[:GW] + energy[1:]) / NS + 1e-05)
                parts.append(raw.reshape(2 * NB, GW, CH) * inv[None])
            both = jnp.concatenate(parts, axis=1).astype(jnp.bfloat16)
            rows = pl.ds(pl.multiple_of(block * WB_ROWS, WB_ROWS), WB_ROWS)
            s_ref[:, rows, :] = both.reshape(8, WB_ROWS, CH)
            return carry

        lax.fori_loop(0, CHUNKS[j][1] // WB_ROWS, run, 0)
        rows = pl.ds(CHUNKS[j][0], CHUNKS[j][1])
        out = pltpu.make_async_copy(s_ref.at[:, rows], own_ref.at[:, rows], isem.at[NCH + j])
        out.start()
        outs.append(out)

    outs = []

    a_copies = [[] for _ in range(NCH)]
    locals_ = [[] for _ in range(NCH)]

    def start_a(j):
        rows = pl.ds(CHUNKS[j][0], CHUNKS[j][1])
        for dz, other in ((2, 0), (2, 1), (1, 0), (3, 0), (1, 1), (3, 1), (0, 1)):
            zz = (z + dz) % 4
            c = 1 - core if other else core
            a_copies[j].append(
                remote(j, s_ref.at[zz * 2 + c, rows], a_buf[j].at[slot], device(0, 0, dz, other))
            )
        own = pltpu.make_async_copy(s_ref.at[slot, rows], a_buf[j].at[slot], lsem.at[j, 0])
        own.start()
        locals_[j].append(own)

    b_copies = [[] for _ in range(NCH)]

    def pick_and_send(j):
        locals_[j][0].wait()
        for cp in a_copies[j]:
            cp.wait_recv()
        w = width(j)
        for r in range(ROUNDS):
            owner = order_ref[r, (blk + r) % 8] % 8

            if r == 0:
                base = pl.multiple_of(xhi * w, 16)

                def keep(at, n, value):
                    b_recv[j][0, xhi, pl.ds(at, n), :] = value

                copy_rows(w, keep, lambda at, n: a_buf[j][owner, pl.ds(base + at, n), :])

            def store(at, n, value):
                b_send[j][r, pl.ds(at, n), :] = value

            copy_rows(CHUNKS[j][1], store, lambda at, n: a_buf[j][owner, pl.ds(at, n), :])
            moves = (
                ((2, 0),),
                ((1, par), (-1, par)),
                ((0, 1), (2, 1)),
                ((1, 1 + par), (-1, 1 + par)),
            )[r]
            for dx, dy in moves:
                column = ((xhi * 2 + par + dx + 4) % 4) // 2
                src = b_send[j].at[r, pl.ds(pl.multiple_of(column * w, 16), w)]
                b_copies[j].append(
                    remote(j, src, b_recv[j].at[r, xhi], device(dx, dy, 0, 0))
                )

    c_copies = [None] * NCH
    x_copies = [[] for _ in range(NCH)]
    sides = []

    def spread(j, zz, src):
        sides.append(remote(j, src, gathered(zz, j), device(0, 0, 0, 1)))
        if CHUNKS[j][2]:
            x_copies[j].append((zz, remote(j, src, place(zz, j, xhi), device(2, 0, 0, 0))))

    def merge(j):
        for cp in b_copies[j]:
            cp.wait_recv()
        for r in range(ROUNDS):
            column = order_ref[r, blk] // 8

            def store(at, n, value):
                final[j][r, pl.ds(at, n), :] = value

            copy_rows(width(j), store, lambda at, n: b_recv[j][r, column, pl.ds(at, n), :])
        own = pltpu.make_async_copy(final[j], place(z, j, xhi), lsem.at[j, 1])
        own.start()
        locals_[j].append(own)
        if CHUNKS[j][2]:
            gather(j, final[j])
        else:
            x_copies[j].append((z, remote(j, final[j], place(z, j, xhi), device(2, 0, 0, 0))))

    def gather(j, src):
        up = remote(j, src, gathered(z, j), device(0, 0, 1, 0))
        down = remote(j, src, gathered(z, j), device(0, 0, -1, 0))
        spread(j, z, src)
        c_copies[j] = [up, down]

    def complete(j):
        x_copies[j][0][1].wait_recv()
        locals_[j][1].wait()
        gather(j, gathered(z, j))

    def forward(j):
        up, down = c_copies[j]
        up.wait_recv()
        part = place(below, j, xhi, 0)
        f_up = remote(j, part, part, device(0, 0, 1, 0))
        spread(j, below, gathered(below, j))
        down.wait_recv()
        part = place(above, j, xhi, 1)
        f_down = remote(j, part, part, device(0, 0, -1, 0))
        spread(j, above, gathered(above, j))
        c_copies[j] = [f_up, f_down]

    def forwarded(j):
        for cp in c_copies[j]:
            cp.wait_recv()
        spread(j, far, gathered(far, j))

    def crossed(j):
        for zz, cp in x_copies[j]:
            cp.wait_recv()
            part = place(zz, j, 1 - xhi)
            sides.append(remote(j, part, part, device(0, 0, 0, 1)))

    steps = {
        True: (pick_and_send, merge, forward, forwarded, crossed),
        False: (pick_and_send, merge, complete, forward, forwarded),
    }
    for j in range(AHEAD):
        compute(j)
        start_a(j)
    for t in range(NCH + max(AGES)):
        if t + AHEAD < NCH:
            compute(t + AHEAD)
        for stage in (4, 3, 2, 1, 0):
            j = t - AGES[stage]
            if 0 <= j < NCH:
                steps[CHUNKS[j][2]][stage](j)
                if stage == 0 and j + AHEAD < NCH:
                    start_a(j + AHEAD)
    for cp in sides:
        cp.wait_recv()
    for j in range(NCH):
        if CHUNKS[j][2]:
            locals_[j][1].wait()
    for cp in everything:
        cp.wait_send()
    for out in outs:
        out.wait()


def exchange(order, record):
    bf16 = jnp.bfloat16
    sizes = [(n, n // 2) for _, n, _ in CHUNKS]
    table = jnp.asarray(banded_table())
    scratch = [pltpu.SMEM(order.shape, order.dtype), pltpu.VMEM(table.shape, bf16)]
    scratch += [pltpu.VMEM(record.shape, bf16), pltpu.VMEM((8, PIECE, CH), bf16)]
    scratch += [pltpu.VMEM((8, n, CH), bf16) for n, _ in sizes]
    scratch += [pltpu.VMEM((ROUNDS, n, CH), bf16) for n, _ in sizes]
    scratch += [pltpu.VMEM((ROUNDS, 2, w, CH), bf16) for _, w in sizes]
    scratch += [pltpu.VMEM((ROUNDS, w, CH), bf16) for _, w in sizes]
    scratch += [
        pltpu.SemaphoreType.DMA((NCH, NSEM)),
        pltpu.SemaphoreType.DMA((NCH, NSEM)),
        pltpu.SemaphoreType.DMA((NCH, 2)),
        pltpu.SemaphoreType.DMA((2 * NCH + 2,)),
    ]
    return pl.pallas_call(
        exchange_kernel,
        out_shape=(
            jax.ShapeDtypeStruct((ROUNDS, 8, PIECE, CH), bf16),
            jax.ShapeDtypeStruct((8, PIECE, CH), bf16),
        ),
        in_specs=[
            pl.BlockSpec(memory_space=pltpu.HBM),
            pl.BlockSpec(memory_space=pltpu.HBM),
            pl.BlockSpec(memory_space=pltpu.HBM),
        ],
        out_specs=(pl.BlockSpec(memory_space=pl.ANY), pl.BlockSpec(memory_space=pl.ANY)),
        scratch_shapes=scratch,
        compiler_params=pltpu.CompilerParams(
            has_side_effects=True, vmem_limit_bytes=26 * 2**20
        ),
        name="exchange",
    )(*(pltpu.with_memory_space_constraint(v, pltpu.HBM) for v in (order, table, record)))


def cross_kernel(own_ref, other_ref, o_ref):
    own = own_ref[0].reshape(WIN // STEPW, 4, STEPW, CH)
    for b in range(2):
        p = own[:, 2 * b].reshape(WIN, CH)
        q = own[:, 2 * b + 1].reshape(WIN, CH)
        pt, qt = p.T, q.T
        left = jnp.concatenate(
            [jnp.concatenate([pt, qt], axis=1), jnp.concatenate([qt, -pt], axis=1)], axis=0
        )
        for r in range(ROUNDS):
            other = other_ref[r, 0].reshape(WIN // STEPW, 4, STEPW, CH)
            right = jnp.concatenate(
                [other[:, 2 * b].reshape(WIN, CH), other[:, 2 * b + 1].reshape(WIN, CH)], axis=0
            )
            out = jnp.dot(left, right, preferred_element_type=jnp.float32)
            out = (out * (1.0 / math.sqrt(WIN))).astype(jnp.bfloat16)
            o_ref[r, 0, b] = out[:CH]
            o_ref[r, 1, b] = out[CH:]


def cross(s, g):
    return pl.pallas_call(
        cross_kernel,
        grid=(8,),
        out_shape=jax.ShapeDtypeStruct((ROUNDS, 2, NB, CH, CH), jnp.bfloat16),
        in_specs=[
            pl.BlockSpec((1, PIECE, CH), lambda f: (f, 0, 0)),
            pl.BlockSpec((ROUNDS, 1, PIECE, CH), lambda f: (0, f, 0, 0)),
        ],
        out_specs=pl.BlockSpec((ROUNDS, 2, 2, CH, CH), lambda f: (0, 0, f, 0, 0)),
        compiler_params=pltpu.CompilerParams(vmem_limit_bytes=12 * 2**20),
        name="cross",
    )(s, g)


def body(record, owner_order):
    g, s = exchange(owner_order, record)
    return cross(s, g)


def solution(mesh):
    placed = (P(None, ("blk", "grp")), P())
    return jax.shard_map(
        body,
        mesh=mesh,
        in_specs=placed,
        out_specs=P(None, None, None, ("blk", "grp"), None),
        check_vma=False,
    )
```

```python
import functools
import math

import jax
import jax.numpy as jnp
import numpy as np
from jax import lax
from jax.experimental import pallas as pl
from jax.experimental.pallas import tpu as pltpu
from jax.sharding import PartitionSpec as P

WIN = 256
NS = 128
NB = 16
BIN_LO = 8
ROUNDS = 4
HOP = 64
CH = 256
GW = 8
STEPW = 16
PIECE = 1024
PLAN = ((2, True), (2, False)) * 4
AHEAD = 2
AGES = (0, 2, 4, 6, 8)
MESH = pl.DeviceIdType.MESH


def band_table():
    sample_index = np.arange(NS, dtype=np.int64)
    bin_index = BIN_LO + np.arange(NB, dtype=np.int64)
    phase = (bin_index[:, None] * sample_index[None, :] % NS) * (2.0 * math.pi / NS)
    taper = 0.5 - 0.5 * np.cos(sample_index * (2.0 * math.pi / NS))
    scale = 1.0 / math.sqrt(3.0 * NS / 8.0)
    real_rows = taper[None, :] * np.cos(phase) * scale
    imag_rows = -taper[None, :] * np.sin(phase) * scale
    return np.stack([real_rows, imag_rows], axis=1).reshape(2 * NB, NS)


def banded_table():
    table = band_table()
    wide = np.zeros((2 * NB, GW, HOP * (GW + 1)), np.float32)
    for w in range(GW):
        wide[:, w, w * HOP : w * HOP + NS] = table
    return wide.reshape(2 * NB * GW, HOP * (GW + 1)).astype(jnp.bfloat16)


NSEM = 32
WB_ROWS = 4 * STEPW
CHUNKS = []
for blocks, shared in PLAN:
    first = CHUNKS[-1][0] + CHUNKS[-1][1] if CHUNKS else 0
    CHUNKS.append((first, blocks * WB_ROWS, shared))
NCH = len(CHUNKS)


def exchange_kernel(order_in, t_in, rec_ref, g_ref, own_ref, *scratch):
    it = iter(scratch)
    order_ref, t_ref = next(it), next(it)
    rec, s_ref = next(it), next(it)
    a_buf = [next(it) for _ in range(NCH)]
    b_send = [next(it) for _ in range(NCH)]
    b_recv = [next(it) for _ in range(NCH)]
    final = [next(it) for _ in range(NCH)]
    ssem, rsem, lsem, isem = next(it), next(it), next(it), next(it)

    blk = lax.axis_index("blk")
    grp = lax.axis_index("grp")
    y, par = blk // 2, blk % 2
    xhi, z, core = grp // 8, (grp // 2) % 4, grp % 2
    slot = z * 2 + core
    below, above, far = (z + 3) % 4, (z + 1) % 4, (z + 2) % 4

    def device(dx, dy, dz, other):
        x = (xhi * 2 + par + dx + 4) % 4
        yy = (y + dy + 4) % 4
        zz = (z + dz + 4) % 4
        c = 1 - core if other else core
        return (yy * 2 + x % 2, (x // 2) * 8 + zz * 2 + c)

    counters = [0] * NCH
    everything = []

    def remote(j, src, dst, target):
        k = counters[j]
        counters[j] += 1
        cp = pltpu.make_async_remote_copy(
            src_ref=src, dst_ref=dst, send_sem=ssem.at[j, k], recv_sem=rsem.at[j, k],
            device_id=target, device_id_type=MESH,
        )
        cp.start()
        everything.append(cp)
        return cp

    def copy_rows(count, store, load):
        step = 32

        def run(i, carry):
            at = pl.multiple_of(i * step, step)
            store(at, step, load(at, step))
            return carry

        lax.fori_loop(0, count // step, run, 0)

    def width(j):
        return CHUNKS[j][1] // 2

    def place(zz, j, column, part=None):
        w = width(j)
        lo = CHUNKS[j][0] + column * w
        if part is not None and CHUNKS[j][2]:
            w = w // 2
            lo = lo + part * w
        elif part is not None:
            lo = CHUNKS[j][0] + part * w
        return g_ref.at[:, zz * 2 + core, pl.ds(pl.multiple_of(lo, 16), w)]

    def gathered(zz, j):
        if CHUNKS[j][2]:
            return place(zz, j, xhi)
        return g_ref.at[:, zz * 2 + core, pl.ds(CHUNKS[j][0], CHUNKS[j][1])]

    small = [
        pltpu.make_async_copy(t_in, t_ref, isem.at[2 * NCH]),
        pltpu.make_async_copy(order_in, order_ref, isem.at[2 * NCH + 1]),
    ]
    small[0].start()
    reads = []
    for j in range(NCH):
        lo = CHUNKS[j][0] // 4 * HOP + (HOP if j else 0)
        hi = (CHUNKS[j][0] + CHUNKS[j][1]) // 4 * HOP + HOP
        rows = pl.ds(lo, hi - lo)
        reads.append(pltpu.make_async_copy(rec_ref.at[rows], rec.at[rows], isem.at[j]))
        reads[j].start()

    small[1].start()

    def compute(j):
        if j == 0:
            small[0].wait()
            small[1].wait()
        reads[j].wait()
        first = CHUNKS[j][0] // WB_ROWS

        def run(i, carry):
            block = first + i
            parts = []
            for half in range(STEPW // GW):
                at = pl.multiple_of(block * (STEPW * HOP) + half * (GW * HOP), HOP)
                x = rec[pl.ds(at, (GW + 1) * HOP), :]
                raw = jnp.dot(t_ref[...], x, preferred_element_type=jnp.float32)
                wide = x.astype(jnp.float32)
                energy = jnp.sum((wide * wide).reshape(GW + 1, HOP, CH), axis=1)
                inv = 1.0 / jnp.sqrt((energy[:GW] + energy[1:]) / NS + 1e-05)
                parts.append(raw.reshape(2 * NB, GW, CH) * inv[None])
            both = jnp.concatenate(parts, axis=1).astype(jnp.bfloat16)
            rows = pl.ds(pl.multiple_of(block * WB_ROWS, WB_ROWS), WB_ROWS)
            s_ref[:, rows, :] = both.reshape(8, WB_ROWS, CH)
            return carry

        lax.fori_loop(0, CHUNKS[j][1] // WB_ROWS, run, 0)
        rows = pl.ds(CHUNKS[j][0], CHUNKS[j][1])
        out = pltpu.make_async_copy(s_ref.at[:, rows], own_ref.at[:, rows], isem.at[NCH + j])
        out.start()
        outs.append(out)

    outs = []

    a_copies = [[] for _ in range(NCH)]
    locals_ = [[] for _ in range(NCH)]

    def start_a(j):
        rows = pl.ds(CHUNKS[j][0], CHUNKS[j][1])
        for dz, other in ((2, 0), (2, 1), (1, 0), (3, 0), (1, 1), (3, 1), (0, 1)):
            zz = (z + dz) % 4
            c = 1 - core if other else core
            a_copies[j].append(
                remote(j, s_ref.at[zz * 2 + c, rows], a_buf[j].at[slot], device(0, 0, dz, other))
            )
        own = pltpu.make_async_copy(s_ref.at[slot, rows], a_buf[j].at[slot], lsem.at[j, 0])
        own.start()
        locals_[j].append(own)

    b_copies = [[] for _ in range(NCH)]

    def pick_and_send(j):
        locals_[j][0].wait()
        for cp in a_copies[j]:
            cp.wait_recv()
        w = width(j)
        for r in range(ROUNDS):
            owner = order_ref[r, (blk + r) % 8] % 8

            if r == 0:
                base = pl.multiple_of(xhi * w, 16)

                def keep(at, n, value):
                    b_recv[j][0, xhi, pl.ds(at, n), :] = value

                copy_rows(w, keep, lambda at, n: a_buf[j][owner, pl.ds(base + at, n), :])

            def store(at, n, value):
                b_send[j][r, pl.ds(at, n), :] = value

            copy_rows(CHUNKS[j][1], store, lambda at, n: a_buf[j][owner, pl.ds(at, n), :])
            moves = (
                ((2, 0),),
                ((1, par), (-1, par)),
                ((0, 1), (2, 1)),
                ((1, 1 + par), (-1, 1 + par)),
            )[r]
            for dx, dy in moves:
                column = ((xhi * 2 + par + dx + 4) % 4) // 2
                src = b_send[j].at[r, pl.ds(pl.multiple_of(column * w, 16), w)]
                b_copies[j].append(
                    remote(j, src, b_recv[j].at[r, xhi], device(dx, dy, 0, 0))
                )

    c_copies = [None] * NCH
    x_copies = [[] for _ in range(NCH)]
    sides = []

    def spread(j, zz, src):
        sides.append(remote(j, src, gathered(zz, j), device(0, 0, 0, 1)))
        if CHUNKS[j][2]:
            x_copies[j].append((zz, remote(j, src, place(zz, j, xhi), device(2, 0, 0, 0))))

    def merge(j):
        for cp in b_copies[j]:
            cp.wait_recv()
        for r in range(ROUNDS):
            column = order_ref[r, blk] // 8

            def store(at, n, value):
                final[j][r, pl.ds(at, n), :] = value

            copy_rows(width(j), store, lambda at, n: b_recv[j][r, column, pl.ds(at, n), :])
        own = pltpu.make_async_copy(final[j], place(z, j, xhi), lsem.at[j, 1])
        own.start()
        locals_[j].append(own)
        if CHUNKS[j][2]:
            gather(j, final[j])
        else:
            x_copies[j].append((z, remote(j, final[j], place(z, j, xhi), device(2, 0, 0, 0))))

    def gather(j, src):
        up = remote(j, src, gathered(z, j), device(0, 0, 1, 0))
        down = remote(j, src, gathered(z, j), device(0, 0, -1, 0))
        spread(j, z, src)
        c_copies[j] = [up, down]

    def complete(j):
        x_copies[j][0][1].wait_recv()
        locals_[j][1].wait()
        gather(j, gathered(z, j))

    def forward(j):
        up, down = c_copies[j]
        up.wait_recv()
        part = place(below, j, xhi, 0)
        f_up = remote(j, part, part, device(0, 0, 1, 0))
        spread(j, below, gathered(below, j))
        down.wait_recv()
        part = place(above, j, xhi, 1)
        f_down = remote(j, part, part, device(0, 0, -1, 0))
        spread(j, above, gathered(above, j))
        c_copies[j] = [f_up, f_down]

    def forwarded(j):
        for cp in c_copies[j]:
            cp.wait_recv()
        spread(j, far, gathered(far, j))

    def crossed(j):
        for zz, cp in x_copies[j]:
            cp.wait_recv()
            part = place(zz, j, 1 - xhi)
            sides.append(remote(j, part, part, device(0, 0, 0, 1)))

    steps = {
        True: (pick_and_send, merge, forward, forwarded, crossed),
        False: (pick_and_send, merge, complete, forward, forwarded),
    }
    for j in range(AHEAD):
        compute(j)
        start_a(j)
    for t in range(NCH + max(AGES)):
        if t + AHEAD < NCH:
            compute(t + AHEAD)
        for stage in (0, 1, 2, 3, 4):
            j = t - AGES[stage]
            if 0 <= j < NCH:
                steps[CHUNKS[j][2]][stage](j)
                if stage == 0 and j + AHEAD < NCH:
                    start_a(j + AHEAD)
    for cp in sides:
        cp.wait_recv()
    for j in range(NCH):
        if CHUNKS[j][2]:
            locals_[j][1].wait()
    for cp in everything:
        cp.wait_send()
    for out in outs:
        out.wait()


def exchange(order, record):
    bf16 = jnp.bfloat16
    sizes = [(n, n // 2) for _, n, _ in CHUNKS]
    table = jnp.asarray(banded_table())
    scratch = [pltpu.SMEM(order.shape, order.dtype), pltpu.VMEM(table.shape, bf16)]
    scratch += [pltpu.VMEM(record.shape, bf16), pltpu.VMEM((8, PIECE, CH), bf16)]
    scratch += [pltpu.VMEM((8, n, CH), bf16) for n, _ in sizes]
    scratch += [pltpu.VMEM((ROUNDS, n, CH), bf16) for n, _ in sizes]
    scratch += [pltpu.VMEM((ROUNDS, 2, w, CH), bf16) for _, w in sizes]
    scratch += [pltpu.VMEM((ROUNDS, w, CH), bf16) for _, w in sizes]
    scratch += [
        pltpu.SemaphoreType.DMA((NCH, NSEM)),
        pltpu.SemaphoreType.DMA((NCH, NSEM)),
        pltpu.SemaphoreType.DMA((NCH, 2)),
        pltpu.SemaphoreType.DMA((2 * NCH + 2,)),
    ]
    return pl.pallas_call(
        exchange_kernel,
        out_shape=(
            jax.ShapeDtypeStruct((ROUNDS, 8, PIECE, CH), bf16),
            jax.ShapeDtypeStruct((8, PIECE, CH), bf16),
        ),
        in_specs=[
            pl.BlockSpec(memory_space=pltpu.HBM),
            pl.BlockSpec(memory_space=pltpu.HBM),
            pl.BlockSpec(memory_space=pltpu.HBM),
        ],
        out_specs=(pl.BlockSpec(memory_space=pl.ANY), pl.BlockSpec(memory_space=pl.ANY)),
        scratch_shapes=scratch,
        compiler_params=pltpu.CompilerParams(
            has_side_effects=True, vmem_limit_bytes=26 * 2**20
        ),
        name="exchange",
    )(*(pltpu.with_memory_space_constraint(v, pltpu.HBM) for v in (order, table, record)))


def cross_kernel(own_ref, other_ref, o_ref):
    piece, parts = pl.program_id(0) // 2, pl.ds(pl.program_id(0) % 2 * 2, 2)
    own = own_ref[piece, :, parts]
    p, q = own[:, 0].reshape(WIN, CH), own[:, 1].reshape(WIN, CH)
    pt, qt = p.T, q.T
    left = jnp.concatenate(
        [jnp.concatenate([pt, qt], axis=1), jnp.concatenate([qt, -pt], axis=1)], axis=0
    )
    for r in range(ROUNDS):
        other = other_ref[r, piece, :, parts]
        right = jnp.concatenate(
            [other[:, 0].reshape(WIN, CH), other[:, 1].reshape(WIN, CH)], axis=0
        )
        out = jnp.dot(left, right, preferred_element_type=jnp.float32)
        out = (out * (1.0 / math.sqrt(WIN))).astype(jnp.bfloat16)
        o_ref[r, 0, 0] = out[:CH]
        o_ref[r, 1, 0] = out[CH:]


def cross(s, g):
    rows = (WIN // STEPW, 4, STEPW, CH)
    return pl.pallas_call(
        cross_kernel,
        grid=(NB,),
        out_shape=jax.ShapeDtypeStruct((ROUNDS, 2, NB, CH, CH), jnp.bfloat16),
        in_specs=[
            pl.BlockSpec(memory_space=pltpu.VMEM),
            pl.BlockSpec(memory_space=pltpu.VMEM),
        ],
        out_specs=pl.BlockSpec((ROUNDS, 2, 1, CH, CH), lambda f: (0, 0, f, 0, 0)),
        compiler_params=pltpu.CompilerParams(vmem_limit_bytes=12 * 2**20),
        name="cross",
    )(s.reshape((8,) + rows), g.reshape((ROUNDS, 8) + rows))


def body(record, owner_order):
    g, s = exchange(owner_order, record)
    return cross(s, g)


def solution(mesh):
    placed = (P(None, ("blk", "grp")), P())
    return jax.shard_map(
        body,
        mesh=mesh,
        in_specs=placed,
        out_specs=P(None, None, None, ("blk", "grp"), None),
        check_vma=False,
    )
```

```python
import functools
import math

import jax
import jax.numpy as jnp
import numpy as np
from jax import lax
from jax.experimental import pallas as pl
from jax.experimental.pallas import tpu as pltpu
from jax.sharding import PartitionSpec as P

WIN = 256
NS = 128
NB = 16
BIN_LO = 8
ROUNDS = 4
HOP = 64
CH = 256
GW = 8
STEPW = 16
PIECE = 1024
PLAN = ((2, True), (2, False)) * 4
AHEAD = 2
AGES = (0, 2, 4, 6, 8)
MESH = pl.DeviceIdType.MESH


def band_table():
    sample_index = np.arange(NS, dtype=np.int64)
    bin_index = BIN_LO + np.arange(NB, dtype=np.int64)
    phase = (bin_index[:, None] * sample_index[None, :] % NS) * (2.0 * math.pi / NS)
    taper = 0.5 - 0.5 * np.cos(sample_index * (2.0 * math.pi / NS))
    scale = 1.0 / math.sqrt(3.0 * NS / 8.0)
    real_rows = taper[None, :] * np.cos(phase) * scale
    imag_rows = -taper[None, :] * np.sin(phase) * scale
    return np.stack([real_rows, imag_rows], axis=1).reshape(2 * NB, NS)


def banded_table():
    table = band_table()
    wide = np.zeros((2 * NB, GW, HOP * (GW + 1)), np.float32)
    for w in range(GW):
        wide[:, w, w * HOP : w * HOP + NS] = table
    return wide.reshape(2 * NB * GW, HOP * (GW + 1)).astype(jnp.bfloat16)


NSEM = 32
WB_ROWS = 4 * STEPW
CHUNKS = []
for blocks, shared in PLAN:
    first = CHUNKS[-1][0] + CHUNKS[-1][1] if CHUNKS else 0
    CHUNKS.append((first, blocks * WB_ROWS, shared))
NCH = len(CHUNKS)


def exchange_kernel(order_in, t_in, rec_ref, g_ref, own_ref, *scratch):
    it = iter(scratch)
    order_ref, t_ref = next(it), next(it)
    rec, s_ref = next(it), next(it)
    a_buf = [next(it) for _ in range(NCH)]
    b_send = [next(it) for _ in range(NCH)]
    b_recv = [next(it) for _ in range(NCH)]
    final = [next(it) for _ in range(NCH)]
    ssem, rsem, lsem, isem = next(it), next(it), next(it), next(it)

    blk = lax.axis_index("blk")
    grp = lax.axis_index("grp")
    y, par = blk // 2, blk % 2
    xhi, z, core = grp // 8, (grp // 2) % 4, grp % 2
    slot = z * 2 + core
    below, above, far = (z + 3) % 4, (z + 1) % 4, (z + 2) % 4

    def device(dx, dy, dz, other):
        x = (xhi * 2 + par + dx + 4) % 4
        yy = (y + dy + 4) % 4
        zz = (z + dz + 4) % 4
        c = 1 - core if other else core
        return (yy * 2 + x % 2, (x // 2) * 8 + zz * 2 + c)

    counters = [0] * NCH
    everything = []

    def remote(j, src, dst, target):
        k = counters[j]
        counters[j] += 1
        cp = pltpu.make_async_remote_copy(
            src_ref=src, dst_ref=dst, send_sem=ssem.at[j, k], recv_sem=rsem.at[j, k],
            device_id=target, device_id_type=MESH,
        )
        cp.start()
        everything.append(cp)
        return cp

    def copy_rows(count, store, load):
        step = 32

        def run(i, carry):
            at = pl.multiple_of(i * step, step)
            store(at, step, load(at, step))
            return carry

        lax.fori_loop(0, count // step, run, 0)

    def width(j):
        return CHUNKS[j][1] // 2

    def place(zz, j, column, part=None):
        w = width(j)
        lo = CHUNKS[j][0] + column * w
        if part is not None and CHUNKS[j][2]:
            w = w // 2
            lo = lo + part * w
        elif part is not None:
            lo = CHUNKS[j][0] + part * w
        return g_ref.at[:, zz * 2 + core, pl.ds(pl.multiple_of(lo, 16), w)]

    def gathered(zz, j):
        if CHUNKS[j][2]:
            return place(zz, j, xhi)
        return g_ref.at[:, zz * 2 + core, pl.ds(CHUNKS[j][0], CHUNKS[j][1])]

    small = [
        pltpu.make_async_copy(t_in, t_ref, isem.at[2 * NCH]),
        pltpu.make_async_copy(order_in, order_ref, isem.at[2 * NCH + 1]),
    ]
    small[0].start()
    reads = []
    for j in range(NCH):
        lo = CHUNKS[j][0] // 4 * HOP + (HOP if j else 0)
        hi = (CHUNKS[j][0] + CHUNKS[j][1]) // 4 * HOP + HOP
        rows = pl.ds(lo, hi - lo)
        reads.append(pltpu.make_async_copy(rec_ref.at[rows], rec.at[rows], isem.at[j]))
        reads[j].start()

    small[1].start()

    def compute(j):
        if j == 0:
            small[0].wait()
            small[1].wait()
        reads[j].wait()
        first = CHUNKS[j][0] // WB_ROWS

        def run(i, carry):
            block = first + i
            parts = []
            for half in range(STEPW // GW):
                at = pl.multiple_of(block * (STEPW * HOP) + half * (GW * HOP), HOP)
                x = rec[pl.ds(at, (GW + 1) * HOP), :]
                raw = jnp.dot(t_ref[...], x, preferred_element_type=jnp.float32)
                wide = x.astype(jnp.float32)
                energy = jnp.sum((wide * wide).reshape(GW + 1, HOP, CH), axis=1)
                inv = 1.0 / jnp.sqrt((energy[:GW] + energy[1:]) / NS + 1e-05)
                parts.append(raw.reshape(2 * NB, GW, CH) * inv[None])
            both = jnp.concatenate(parts, axis=1).astype(jnp.bfloat16)
            rows = pl.ds(pl.multiple_of(block * WB_ROWS, WB_ROWS), WB_ROWS)
            s_ref[:, rows, :] = both.reshape(8, WB_ROWS, CH)
            return carry

        lax.fori_loop(0, CHUNKS[j][1] // WB_ROWS, run, 0)
        rows = pl.ds(CHUNKS[j][0], CHUNKS[j][1])
        out = pltpu.make_async_copy(s_ref.at[:, rows], own_ref.at[:, rows], isem.at[NCH + j])
        out.start()
        outs.append(out)

    outs = []

    a_copies = [[] for _ in range(NCH)]
    locals_ = [[] for _ in range(NCH)]

    def start_a(j):
        rows = pl.ds(CHUNKS[j][0], CHUNKS[j][1])
        for dz, other in ((2, 0), (2, 1), (1, 0), (3, 0), (1, 1), (3, 1), (0, 1)):
            zz = (z + dz) % 4
            c = 1 - core if other else core
            a_copies[j].append(
                remote(j, s_ref.at[zz * 2 + c, rows], a_buf[j].at[slot], device(0, 0, dz, other))
            )
        own = pltpu.make_async_copy(s_ref.at[slot, rows], a_buf[j].at[slot], lsem.at[j, 0])
        own.start()
        locals_[j].append(own)

    b_copies = [[] for _ in range(NCH)]

    def pick_and_send(j):
        locals_[j][0].wait()
        for cp in a_copies[j]:
            cp.wait_recv()
        w = width(j)
        for r in range(ROUNDS):
            owner = order_ref[r, (blk + r) % 8] % 8

            if r == 0:
                base = pl.multiple_of(xhi * w, 16)

                def keep(at, n, value):
                    b_recv[j][0, xhi, pl.ds(at, n), :] = value

                copy_rows(w, keep, lambda at, n: a_buf[j][owner, pl.ds(base + at, n), :])

            def store(at, n, value):
                b_send[j][r, pl.ds(at, n), :] = value

            copy_rows(CHUNKS[j][1], store, lambda at, n: a_buf[j][owner, pl.ds(at, n), :])
            moves = (
                ((2, 0),),
                ((1, par), (-1, par)),
                ((0, 1), (2, 1)),
                ((1, 1 + par), (-1, 1 + par)),
            )[r]
            for dx, dy in moves:
                column = ((xhi * 2 + par + dx + 4) % 4) // 2
                src = b_send[j].at[r, pl.ds(pl.multiple_of(column * w, 16), w)]
                b_copies[j].append(
                    remote(j, src, b_recv[j].at[r, xhi], device(dx, dy, 0, 0))
                )

    c_copies = [None] * NCH
    x_copies = [[] for _ in range(NCH)]
    sides = []

    def spread(j, zz, src):
        sides.append(remote(j, src, gathered(zz, j), device(0, 0, 0, 1)))
        if CHUNKS[j][2]:
            x_copies[j].append((zz, remote(j, src, place(zz, j, xhi), device(2, 0, 0, 0))))

    def merge(j):
        for cp in b_copies[j]:
            cp.wait_recv()
        for r in range(ROUNDS):
            column = order_ref[r, blk] // 8

            def store(at, n, value):
                final[j][r, pl.ds(at, n), :] = value

            copy_rows(width(j), store, lambda at, n: b_recv[j][r, column, pl.ds(at, n), :])
        own = pltpu.make_async_copy(final[j], place(z, j, xhi), lsem.at[j, 1])
        own.start()
        locals_[j].append(own)
        if CHUNKS[j][2]:
            gather(j, final[j])
        else:
            x_copies[j].append((z, remote(j, final[j], place(z, j, xhi), device(2, 0, 0, 0))))

    def gather(j, src):
        up = remote(j, src, gathered(z, j), device(0, 0, 1, 0))
        down = remote(j, src, gathered(z, j), device(0, 0, -1, 0))
        spread(j, z, src)
        c_copies[j] = [up, down]

    def complete(j):
        x_copies[j][0][1].wait_recv()
        locals_[j][1].wait()
        gather(j, gathered(z, j))

    def forward(j):
        up, down = c_copies[j]
        up.wait_recv()
        part = place(below, j, xhi, 0)
        f_up = remote(j, part, part, device(0, 0, 1, 0))
        spread(j, below, gathered(below, j))
        down.wait_recv()
        part = place(above, j, xhi, 1)
        f_down = remote(j, part, part, device(0, 0, -1, 0))
        spread(j, above, gathered(above, j))
        c_copies[j] = [f_up, f_down]

    def forwarded(j):
        for cp in c_copies[j]:
            cp.wait_recv()
        spread(j, far, gathered(far, j))

    def crossed(j):
        for zz, cp in x_copies[j]:
            cp.wait_recv()
            part = place(zz, j, 1 - xhi)
            sides.append(remote(j, part, part, device(0, 0, 0, 1)))

    steps = {
        True: (pick_and_send, merge, forward, forwarded, crossed),
        False: (pick_and_send, merge, complete, forward, forwarded),
    }
    for j in range(AHEAD):
        compute(j)
        start_a(j)
    for t in range(NCH + max(AGES)):
        if t + AHEAD < NCH:
            compute(t + AHEAD)
        for stage in (0, 1, 2, 3, 4):
            j = t - AGES[stage]
            if 0 <= j < NCH:
                steps[CHUNKS[j][2]][stage](j)
                if stage == 0 and j + AHEAD < NCH:
                    start_a(j + AHEAD)
    for cp in sides:
        cp.wait_recv()
    for j in range(NCH):
        if CHUNKS[j][2]:
            locals_[j][1].wait()
    for cp in everything:
        cp.wait_send()
    for out in outs:
        out.wait()


def exchange(order, record):
    bf16 = jnp.bfloat16
    sizes = [(n, n // 2) for _, n, _ in CHUNKS]
    table = jnp.asarray(banded_table())
    scratch = [pltpu.SMEM(order.shape, order.dtype), pltpu.VMEM(table.shape, bf16)]
    scratch += [pltpu.VMEM(record.shape, bf16), pltpu.VMEM((8, PIECE, CH), bf16)]
    scratch += [pltpu.VMEM((8, n, CH), bf16) for n, _ in sizes]
    scratch += [pltpu.VMEM((ROUNDS, n, CH), bf16) for n, _ in sizes]
    scratch += [pltpu.VMEM((ROUNDS, 2, w, CH), bf16) for _, w in sizes]
    scratch += [pltpu.VMEM((ROUNDS, w, CH), bf16) for _, w in sizes]
    scratch += [
        pltpu.SemaphoreType.DMA((NCH, NSEM)),
        pltpu.SemaphoreType.DMA((NCH, NSEM)),
        pltpu.SemaphoreType.DMA((NCH, 2)),
        pltpu.SemaphoreType.DMA((2 * NCH + 2,)),
    ]
    return pl.pallas_call(
        exchange_kernel,
        out_shape=(
            jax.ShapeDtypeStruct((ROUNDS, 8, PIECE, CH), bf16),
            jax.ShapeDtypeStruct((8, PIECE, CH), bf16),
        ),
        in_specs=[
            pl.BlockSpec(memory_space=pltpu.HBM),
            pl.BlockSpec(memory_space=pltpu.HBM),
            pl.BlockSpec(memory_space=pltpu.HBM),
        ],
        out_specs=(pl.BlockSpec(memory_space=pl.ANY), pl.BlockSpec(memory_space=pl.ANY)),
        scratch_shapes=scratch,
        compiler_params=pltpu.CompilerParams(
            has_side_effects=True, vmem_limit_bytes=26 * 2**20
        ),
        name="exchange",
    )(*(pltpu.with_memory_space_constraint(v, pltpu.HBM) for v in (order, table, record)))


def cross_kernel(own_ref, other_ref, o_ref):
    piece = pl.program_id(0)
    own = own_ref[piece].reshape(WIN // STEPW, 4, STEPW, CH)
    for b in range(2):
        p = own[:, 2 * b].reshape(WIN, CH)
        q = own[:, 2 * b + 1].reshape(WIN, CH)
        pt, qt = p.T, q.T
        left = jnp.concatenate(
            [jnp.concatenate([pt, qt], axis=1), jnp.concatenate([qt, -pt], axis=1)], axis=0
        )
        for r in range(ROUNDS):
            other = other_ref[r, piece].reshape(WIN // STEPW, 4, STEPW, CH)
            right = jnp.concatenate(
                [other[:, 2 * b].reshape(WIN, CH), other[:, 2 * b + 1].reshape(WIN, CH)], axis=0
            )
            out = jnp.dot(left, right, preferred_element_type=jnp.float32)
            out = (out * (1.0 / math.sqrt(WIN))).astype(jnp.bfloat16)
            o_ref[r, 0, b] = out[:CH]
            o_ref[r, 1, b] = out[CH:]


def cross(s, g):
    return pl.pallas_call(
        cross_kernel,
        grid=(8,),
        out_shape=jax.ShapeDtypeStruct((ROUNDS, 2, NB, CH, CH), jnp.bfloat16),
        in_specs=[
            pl.BlockSpec(memory_space=pltpu.VMEM),
            pl.BlockSpec(memory_space=pltpu.VMEM),
        ],
        out_specs=pl.BlockSpec((ROUNDS, 2, 2, CH, CH), lambda f: (0, 0, f, 0, 0)),
        compiler_params=pltpu.CompilerParams(vmem_limit_bytes=12 * 2**20),
        name="cross",
    )(s, g)


def body(record, owner_order):
    g, s = exchange(owner_order, record)
    return cross(s, g)


def solution(mesh):
    placed = (P(None, ("blk", "grp")), P())
    return jax.shard_map(
        body,
        mesh=mesh,
        in_specs=placed,
        out_specs=P(None, None, None, ("blk", "grp"), None),
        check_vma=False,
    )
```

```python
import functools
import math

import jax
import jax.numpy as jnp
import numpy as np
from jax import lax
from jax.experimental import pallas as pl
from jax.experimental.pallas import tpu as pltpu
from jax.sharding import PartitionSpec as P

WIN = 256
NS = 128
NB = 16
BIN_LO = 8
ROUNDS = 4
HOP = 64
CH = 256
GW = 8
STEPW = 16
PIECE = 1024
PLAN = ((2, True), (2, False)) * 4
AHEAD = 2
AGES = (0, 2, 4, 6, 8)
MESH = pl.DeviceIdType.MESH


def band_table():
    sample_index = np.arange(NS, dtype=np.int64)
    bin_index = BIN_LO + np.arange(NB, dtype=np.int64)
    phase = (bin_index[:, None] * sample_index[None, :] % NS) * (2.0 * math.pi / NS)
    taper = 0.5 - 0.5 * np.cos(sample_index * (2.0 * math.pi / NS))
    scale = 1.0 / math.sqrt(3.0 * NS / 8.0)
    real_rows = taper[None, :] * np.cos(phase) * scale
    imag_rows = -taper[None, :] * np.sin(phase) * scale
    return np.stack([real_rows, imag_rows], axis=1).reshape(2 * NB, NS)


def banded_table():
    table = band_table()
    wide = np.zeros((2 * NB, GW, HOP * (GW + 1)), np.float32)
    for w in range(GW):
        wide[:, w, w * HOP : w * HOP + NS] = table
    return wide.reshape(2 * NB * GW, HOP * (GW + 1)).astype(jnp.bfloat16)


NSEM = 32
WB_ROWS = 4 * STEPW
CHUNKS = []
for blocks, shared in PLAN:
    first = CHUNKS[-1][0] + CHUNKS[-1][1] if CHUNKS else 0
    CHUNKS.append((first, blocks * WB_ROWS, shared))
NCH = len(CHUNKS)


def exchange_kernel(order_in, t_in, rec_ref, g_ref, own_ref, *scratch):
    it = iter(scratch)
    order_ref, t_ref = next(it), next(it)
    rec, s_ref = next(it), next(it)
    a_buf = [next(it) for _ in range(NCH)]
    b_send = [next(it) for _ in range(NCH)]
    b_recv = [next(it) for _ in range(NCH)]
    final = [next(it) for _ in range(NCH)]
    ssem, rsem, lsem, isem = next(it), next(it), next(it), next(it)

    blk = lax.axis_index("blk")
    grp = lax.axis_index("grp")
    y, par = blk // 2, blk % 2
    xhi, z, core = grp // 8, (grp // 2) % 4, grp % 2
    slot = z * 2 + core
    below, above, far = (z + 3) % 4, (z + 1) % 4, (z + 2) % 4

    def device(dx, dy, dz, other):
        x = (xhi * 2 + par + dx + 4) % 4
        yy = (y + dy + 4) % 4
        zz = (z + dz + 4) % 4
        c = 1 - core if other else core
        return (yy * 2 + x % 2, (x // 2) * 8 + zz * 2 + c)

    counters = [0] * NCH
    everything = []

    def remote(j, src, dst, target):
        k = counters[j]
        counters[j] += 1
        cp = pltpu.make_async_remote_copy(
            src_ref=src, dst_ref=dst, send_sem=ssem.at[j, k], recv_sem=rsem.at[j, k],
            device_id=target, device_id_type=MESH,
        )
        cp.start()
        everything.append(cp)
        return cp

    def copy_rows(count, store, load):
        step = 32

        def run(i, carry):
            at = pl.multiple_of(i * step, step)
            store(at, step, load(at, step))
            return carry

        lax.fori_loop(0, count // step, run, 0)

    def width(j):
        return CHUNKS[j][1] // 2

    def place(zz, j, column, part=None):
        w = width(j)
        lo = CHUNKS[j][0] + column * w
        if part is not None and CHUNKS[j][2]:
            w = w // 2
            lo = lo + part * w
        elif part is not None:
            lo = CHUNKS[j][0] + part * w
        return g_ref.at[:, zz * 2 + core, pl.ds(pl.multiple_of(lo, 16), w)]

    def gathered(zz, j):
        if CHUNKS[j][2]:
            return place(zz, j, xhi)
        return g_ref.at[:, zz * 2 + core, pl.ds(CHUNKS[j][0], CHUNKS[j][1])]

    small = [
        pltpu.make_async_copy(t_in, t_ref, isem.at[2 * NCH]),
        pltpu.make_async_copy(order_in, order_ref, isem.at[2 * NCH + 1]),
    ]
    small[0].start()
    reads = []
    for j in range(NCH):
        lo = CHUNKS[j][0] // 4 * HOP + (HOP if j else 0)
        hi = (CHUNKS[j][0] + CHUNKS[j][1]) // 4 * HOP + HOP
        rows = pl.ds(lo, hi - lo)
        reads.append(pltpu.make_async_copy(rec_ref.at[rows], rec.at[rows], isem.at[j]))
        reads[j].start()

    small[1].start()

    def compute(j):
        if j == 0:
            small[0].wait()
            small[1].wait()
        reads[j].wait()
        first = CHUNKS[j][0] // WB_ROWS

        def run(i, carry):
            block = first + i
            parts = []
            for half in range(STEPW // GW):
                at = pl.multiple_of(block * (STEPW * HOP) + half * (GW * HOP), HOP)
                x = rec[pl.ds(at, (GW + 1) * HOP), :]
                raw = jnp.dot(t_ref[...], x, preferred_element_type=jnp.float32)
                wide = x.astype(jnp.float32)
                energy = jnp.sum((wide * wide).reshape(GW + 1, HOP, CH), axis=1)
                inv = 1.0 / jnp.sqrt((energy[:GW] + energy[1:]) / NS + 1e-05)
                parts.append(raw.reshape(2 * NB, GW, CH) * inv[None])
            both = jnp.concatenate(parts, axis=1).astype(jnp.bfloat16)
            rows = pl.ds(pl.multiple_of(block * WB_ROWS, WB_ROWS), WB_ROWS)
            s_ref[:, rows, :] = both.reshape(8, WB_ROWS, CH)
            return carry

        lax.fori_loop(0, CHUNKS[j][1] // WB_ROWS, run, 0)
        rows = pl.ds(CHUNKS[j][0], CHUNKS[j][1])
        out = pltpu.make_async_copy(s_ref.at[:, rows], own_ref.at[:, rows], isem.at[NCH + j])
        out.start()
        outs.append(out)

    outs = []

    a_copies = [[] for _ in range(NCH)]
    locals_ = [[] for _ in range(NCH)]

    def start_a(j):
        rows = pl.ds(CHUNKS[j][0], CHUNKS[j][1])
        for dz, other in ((2, 0), (2, 1), (1, 0), (3, 0), (1, 1), (3, 1), (0, 1)):
            zz = (z + dz) % 4
            c = 1 - core if other else core
            a_copies[j].append(
                remote(j, s_ref.at[zz * 2 + c, rows], a_buf[j].at[slot], device(0, 0, dz, other))
            )
        own = pltpu.make_async_copy(s_ref.at[slot, rows], a_buf[j].at[slot], lsem.at[j, 0])
        own.start()
        locals_[j].append(own)

    b_copies = [[] for _ in range(NCH)]

    def pick_and_send(j):
        locals_[j][0].wait()
        for cp in a_copies[j]:
            cp.wait_recv()
        w = width(j)
        for r in range(ROUNDS):
            owner = order_ref[r, (blk + r) % 8] % 8

            if r == 0:
                base = pl.multiple_of(xhi * w, 16)

                def keep(at, n, value):
                    b_recv[j][0, xhi, pl.ds(at, n), :] = value

                copy_rows(w, keep, lambda at, n: a_buf[j][owner, pl.ds(base + at, n), :])

            def store(at, n, value):
                b_send[j][r, pl.ds(at, n), :] = value

            copy_rows(CHUNKS[j][1], store, lambda at, n: a_buf[j][owner, pl.ds(at, n), :])
            moves = (
                ((2, 0),),
                ((1, par), (-1, par)),
                ((0, 1), (2, 1)),
                ((1, 1 + par), (-1, 1 + par)),
            )[r]
            for dx, dy in moves:
                column = ((xhi * 2 + par + dx + 4) % 4) // 2
                src = b_send[j].at[r, pl.ds(pl.multiple_of(column * w, 16), w)]
                b_copies[j].append(
                    remote(j, src, b_recv[j].at[r, xhi], device(dx, dy, 0, 0))
                )

    c_copies = [None] * NCH
    x_copies = [[] for _ in range(NCH)]
    sides = []

    def spread(j, zz, src):
        sides.append(remote(j, src, gathered(zz, j), device(0, 0, 0, 1)))
        if CHUNKS[j][2]:
            x_copies[j].append((zz, remote(j, src, place(zz, j, xhi), device(2, 0, 0, 0))))

    def merge(j):
        for cp in b_copies[j]:
            cp.wait_recv()
        for r in range(ROUNDS):
            column = order_ref[r, blk] // 8

            def store(at, n, value):
                final[j][r, pl.ds(at, n), :] = value

            copy_rows(width(j), store, lambda at, n: b_recv[j][r, column, pl.ds(at, n), :])
        own = pltpu.make_async_copy(final[j], place(z, j, xhi), lsem.at[j, 1])
        own.start()
        locals_[j].append(own)
        if CHUNKS[j][2]:
            gather(j, final[j])
        else:
            x_copies[j].append((z, remote(j, final[j], place(z, j, xhi), device(2, 0, 0, 0))))

    def gather(j, src):
        up = remote(j, src, gathered(z, j), device(0, 0, 1, 0))
        down = remote(j, src, gathered(z, j), device(0, 0, -1, 0))
        spread(j, z, src)
        c_copies[j] = [up, down]

    def complete(j):
        x_copies[j][0][1].wait_recv()
        locals_[j][1].wait()
        gather(j, gathered(z, j))

    def forward(j):
        up, down = c_copies[j]
        up.wait_recv()
        part = place(below, j, xhi, 0)
        f_up = remote(j, part, part, device(0, 0, 1, 0))
        spread(j, below, gathered(below, j))
        down.wait_recv()
        part = place(above, j, xhi, 1)
        f_down = remote(j, part, part, device(0, 0, -1, 0))
        spread(j, above, gathered(above, j))
        c_copies[j] = [f_up, f_down]

    def forwarded(j):
        for cp in c_copies[j]:
            cp.wait_recv()
        spread(j, far, gathered(far, j))

    def crossed(j):
        for zz, cp in x_copies[j]:
            cp.wait_recv()
            part = place(zz, j, 1 - xhi)
            sides.append(remote(j, part, part, device(0, 0, 0, 1)))

    steps = {
        True: (pick_and_send, merge, forward, forwarded, crossed),
        False: (pick_and_send, merge, complete, forward, forwarded),
    }
    for j in range(AHEAD):
        compute(j)
        start_a(j)
    for t in range(NCH + max(AGES)):
        if t + AHEAD < NCH:
            compute(t + AHEAD)
        for stage in (0, 1, 2, 3, 4):
            j = t - AGES[stage]
            if 0 <= j < NCH:
                steps[CHUNKS[j][2]][stage](j)
                if stage == 0 and j + AHEAD < NCH:
                    start_a(j + AHEAD)
    for cp in sides:
        cp.wait_recv()
    for j in range(NCH):
        if CHUNKS[j][2]:
            locals_[j][1].wait()
    for cp in everything:
        cp.wait_send()
    for out in outs:
        out.wait()


def exchange(order, record):
    bf16 = jnp.bfloat16
    sizes = [(n, n // 2) for _, n, _ in CHUNKS]
    table = jnp.asarray(banded_table())
    scratch = [pltpu.SMEM(order.shape, order.dtype), pltpu.VMEM(table.shape, bf16)]
    scratch += [pltpu.VMEM(record.shape, bf16), pltpu.VMEM((8, PIECE, CH), bf16)]
    scratch += [pltpu.VMEM((8, n, CH), bf16) for n, _ in sizes]
    scratch += [pltpu.VMEM((ROUNDS, n, CH), bf16) for n, _ in sizes]
    scratch += [pltpu.VMEM((ROUNDS, 2, w, CH), bf16) for _, w in sizes]
    scratch += [pltpu.VMEM((ROUNDS, w, CH), bf16) for _, w in sizes]
    scratch += [
        pltpu.SemaphoreType.DMA((NCH, NSEM)),
        pltpu.SemaphoreType.DMA((NCH, NSEM)),
        pltpu.SemaphoreType.DMA((NCH, 2)),
        pltpu.SemaphoreType.DMA((2 * NCH + 2,)),
    ]
    return pl.pallas_call(
        exchange_kernel,
        out_shape=(
            jax.ShapeDtypeStruct((ROUNDS, 8, PIECE, CH), bf16),
            jax.ShapeDtypeStruct((8, PIECE, CH), bf16),
        ),
        in_specs=[
            pl.BlockSpec(memory_space=pltpu.HBM),
            pl.BlockSpec(memory_space=pltpu.HBM),
            pl.BlockSpec(memory_space=pltpu.HBM),
        ],
        out_specs=(pl.BlockSpec(memory_space=pl.ANY), pl.BlockSpec(memory_space=pl.ANY)),
        scratch_shapes=scratch,
        compiler_params=pltpu.CompilerParams(
            has_side_effects=True, vmem_limit_bytes=26 * 2**20
        ),
        name="exchange",
    )(*(pltpu.with_memory_space_constraint(v, pltpu.HBM) for v in (order, table, record)))


def cross_kernel(own_ref, other_ref, o_ref):
    piece = pl.program_id(0)
    scale = jnp.bfloat16(1.0 / math.sqrt(WIN))
    own = own_ref[piece].reshape(WIN // STEPW, 4, STEPW, CH)
    for b in range(2):
        p = own[:, 2 * b].reshape(WIN, CH)
        q = own[:, 2 * b + 1].reshape(WIN, CH)
        pt, qt = p.T * scale, q.T * scale
        left = jnp.concatenate(
            [jnp.concatenate([pt, qt], axis=1), jnp.concatenate([qt, -pt], axis=1)], axis=0
        )
        for r in range(ROUNDS):
            other = other_ref[r, piece].reshape(WIN // STEPW, 4, STEPW, CH)
            right = jnp.concatenate(
                [other[:, 2 * b].reshape(WIN, CH), other[:, 2 * b + 1].reshape(WIN, CH)], axis=0
            )
            out = jnp.dot(left, right, preferred_element_type=jnp.float32)
            out = out.astype(jnp.bfloat16)
            o_ref[r, 0, b] = out[:CH]
            o_ref[r, 1, b] = out[CH:]


def cross(s, g):
    return pl.pallas_call(
        cross_kernel,
        grid=(8,),
        out_shape=jax.ShapeDtypeStruct((ROUNDS, 2, NB, CH, CH), jnp.bfloat16),
        in_specs=[
            pl.BlockSpec(memory_space=pltpu.VMEM),
            pl.BlockSpec(memory_space=pltpu.VMEM),
        ],
        out_specs=pl.BlockSpec((ROUNDS, 2, 2, CH, CH), lambda f: (0, 0, f, 0, 0)),
        compiler_params=pltpu.CompilerParams(vmem_limit_bytes=12 * 2**20),
        name="cross",
    )(s, g)


def body(record, owner_order):
    g, s = exchange(owner_order, record)
    return cross(s, g)


def solution(mesh):
    placed = (P(None, ("blk", "grp")), P())
    return jax.shard_map(
        body,
        mesh=mesh,
        in_specs=placed,
        out_specs=P(None, None, None, ("blk", "grp"), None),
        check_vma=False,
    )
```

```python
import functools
import math

import jax
import jax.numpy as jnp
import numpy as np
from jax import lax
from jax.experimental import pallas as pl
from jax.experimental.pallas import tpu as pltpu
from jax.sharding import PartitionSpec as P

WIN = 256
NS = 128
NB = 16
BIN_LO = 8
ROUNDS = 4
HOP = 64
CH = 256
GW = 8
STEPW = 16
PIECE = 1024
PLAN = ((2, True), (2, False)) * 4
AHEAD = 2
AGES = (0, 2, 4, 6, 8)
MESH = pl.DeviceIdType.MESH


def band_table():
    sample_index = np.arange(NS, dtype=np.int64)
    bin_index = BIN_LO + np.arange(NB, dtype=np.int64)
    phase = (bin_index[:, None] * sample_index[None, :] % NS) * (2.0 * math.pi / NS)
    taper = 0.5 - 0.5 * np.cos(sample_index * (2.0 * math.pi / NS))
    scale = 1.0 / math.sqrt(3.0 * NS / 8.0)
    real_rows = taper[None, :] * np.cos(phase) * scale
    imag_rows = -taper[None, :] * np.sin(phase) * scale
    return np.stack([real_rows, imag_rows], axis=1).reshape(2 * NB, NS)


def banded_table():
    table = band_table()
    wide = np.zeros((2 * NB, GW, HOP * (GW + 1)), np.float32)
    for w in range(GW):
        wide[:, w, w * HOP : w * HOP + NS] = table
    return wide.reshape(2 * NB * GW, HOP * (GW + 1)).astype(jnp.bfloat16)


NSEM = 32
WB_ROWS = 4 * STEPW
CHUNKS = []
for blocks, shared in PLAN:
    first = CHUNKS[-1][0] + CHUNKS[-1][1] if CHUNKS else 0
    CHUNKS.append((first, blocks * WB_ROWS, shared))
NCH = len(CHUNKS)


def exchange_kernel(order_in, t_in, rec_ref, g_ref, own_ref, *scratch):
    it = iter(scratch)
    order_ref, t_ref = next(it), next(it)
    rec, s_ref = next(it), next(it)
    a_buf = [next(it) for _ in range(NCH)]
    b_send = [next(it) for _ in range(NCH)]
    b_recv = [next(it) for _ in range(NCH)]
    final = [next(it) for _ in range(NCH)]
    ssem, rsem, lsem, isem = next(it), next(it), next(it), next(it)

    blk = lax.axis_index("blk")
    grp = lax.axis_index("grp")
    y, par = blk // 2, blk % 2
    xhi, z, core = grp // 8, (grp // 2) % 4, grp % 2
    slot = z * 2 + core
    below, above, far = (z + 3) % 4, (z + 1) % 4, (z + 2) % 4

    def device(dx, dy, dz, other):
        x = (xhi * 2 + par + dx + 4) % 4
        yy = (y + dy + 4) % 4
        zz = (z + dz + 4) % 4
        c = 1 - core if other else core
        return (yy * 2 + x % 2, (x // 2) * 8 + zz * 2 + c)

    counters = [0] * NCH
    everything = []

    def remote(j, src, dst, target):
        k = counters[j]
        counters[j] += 1
        cp = pltpu.make_async_remote_copy(
            src_ref=src, dst_ref=dst, send_sem=ssem.at[j, k], recv_sem=rsem.at[j, k],
            device_id=target, device_id_type=MESH,
        )
        cp.start()
        everything.append(cp)
        return cp

    def copy_rows(count, store, load):
        step = 32

        def run(i, carry):
            at = pl.multiple_of(i * step, step)
            store(at, step, load(at, step))
            return carry

        lax.fori_loop(0, count // step, run, 0)

    def width(j):
        return CHUNKS[j][1] // 2

    def place(zz, j, column, part=None):
        w = width(j)
        lo = CHUNKS[j][0] + column * w
        if part is not None and CHUNKS[j][2]:
            w = w // 2
            lo = lo + part * w
        elif part is not None:
            lo = CHUNKS[j][0] + part * w
        return g_ref.at[:, zz * 2 + core, pl.ds(pl.multiple_of(lo, 16), w)]

    def gathered(zz, j):
        if CHUNKS[j][2]:
            return place(zz, j, xhi)
        return g_ref.at[:, zz * 2 + core, pl.ds(CHUNKS[j][0], CHUNKS[j][1])]

    small = [
        pltpu.make_async_copy(t_in, t_ref, isem.at[2 * NCH]),
        pltpu.make_async_copy(order_in, order_ref, isem.at[2 * NCH + 1]),
    ]
    small[0].start()
    reads = []
    for j in range(NCH):
        lo = CHUNKS[j][0] // 4 * HOP + (HOP if j else 0)
        hi = (CHUNKS[j][0] + CHUNKS[j][1]) // 4 * HOP + HOP
        rows = pl.ds(lo, hi - lo)
        reads.append(pltpu.make_async_copy(rec_ref.at[rows], rec.at[rows], isem.at[j]))
        reads[j].start()

    small[1].start()

    def compute(j):
        if j == 0:
            small[0].wait()
            small[1].wait()
        reads[j].wait()
        first = CHUNKS[j][0] // WB_ROWS

        def run(i, carry):
            block = first + i
            parts = []
            for half in range(STEPW // GW):
                at = pl.multiple_of(block * (STEPW * HOP) + half * (GW * HOP), HOP)
                x = rec[pl.ds(at, (GW + 1) * HOP), :]
                raw = jnp.dot(t_ref[...], x, preferred_element_type=jnp.float32)
                wide = x.astype(jnp.float32)
                energy = jnp.sum((wide * wide).reshape(GW + 1, HOP, CH), axis=1)
                inv = 1.0 / jnp.sqrt((energy[:GW] + energy[1:]) / NS + 1e-05)
                parts.append(raw.reshape(2 * NB, GW, CH) * inv[None])
            both = jnp.concatenate(parts, axis=1).astype(jnp.bfloat16)
            rows = pl.ds(pl.multiple_of(block * WB_ROWS, WB_ROWS), WB_ROWS)
            s_ref[:, rows, :] = both.reshape(8, WB_ROWS, CH)
            return carry

        lax.fori_loop(0, CHUNKS[j][1] // WB_ROWS, run, 0)
        rows = pl.ds(CHUNKS[j][0], CHUNKS[j][1])
        out = pltpu.make_async_copy(s_ref.at[:, rows], own_ref.at[:, rows], isem.at[NCH + j])
        out.start()
        outs.append(out)

    outs = []

    a_copies = [[] for _ in range(NCH)]
    locals_ = [[] for _ in range(NCH)]

    def start_a(j):
        rows = pl.ds(CHUNKS[j][0], CHUNKS[j][1])
        for dz, other in ((2, 0), (2, 1), (1, 0), (3, 0), (1, 1), (3, 1), (0, 1)):
            zz = (z + dz) % 4
            c = 1 - core if other else core
            a_copies[j].append(
                remote(j, s_ref.at[zz * 2 + c, rows], a_buf[j].at[slot], device(0, 0, dz, other))
            )
        own = pltpu.make_async_copy(s_ref.at[slot, rows], a_buf[j].at[slot], lsem.at[j, 0])
        own.start()
        locals_[j].append(own)

    b_copies = [[] for _ in range(NCH)]

    def pick_and_send(j):
        locals_[j][0].wait()
        for cp in a_copies[j]:
            cp.wait_recv()
        w = width(j)
        for r in (3, 1, 2, 0):
            owner = order_ref[r, (blk + r) % 8] % 8

            if r == 0:
                base = pl.multiple_of(xhi * w, 16)

                def keep(at, n, value):
                    b_recv[j][0, xhi, pl.ds(at, n), :] = value

                copy_rows(w, keep, lambda at, n: a_buf[j][owner, pl.ds(base + at, n), :])

            def store(at, n, value):
                b_send[j][r, pl.ds(at, n), :] = value

            copy_rows(CHUNKS[j][1], store, lambda at, n: a_buf[j][owner, pl.ds(at, n), :])
            moves = (
                ((2, 0),),
                ((1, par), (-1, par)),
                ((0, 1), (2, 1)),
                ((1, 1 + par), (-1, 1 + par)),
            )[r]
            for dx, dy in moves:
                column = ((xhi * 2 + par + dx + 4) % 4) // 2
                src = b_send[j].at[r, pl.ds(pl.multiple_of(column * w, 16), w)]
                b_copies[j].append(
                    remote(j, src, b_recv[j].at[r, xhi], device(dx, dy, 0, 0))
                )

    c_copies = [None] * NCH
    x_copies = [[] for _ in range(NCH)]
    sides = []

    def spread(j, zz, src):
        sides.append(remote(j, src, gathered(zz, j), device(0, 0, 0, 1)))
        if CHUNKS[j][2]:
            x_copies[j].append((zz, remote(j, src, place(zz, j, xhi), device(2, 0, 0, 0))))

    def merge(j):
        for cp in b_copies[j]:
            cp.wait_recv()
        for r in range(ROUNDS):
            column = order_ref[r, blk] // 8

            def store(at, n, value):
                final[j][r, pl.ds(at, n), :] = value

            copy_rows(width(j), store, lambda at, n: b_recv[j][r, column, pl.ds(at, n), :])
        own = pltpu.make_async_copy(final[j], place(z, j, xhi), lsem.at[j, 1])
        own.start()
        locals_[j].append(own)
        if CHUNKS[j][2]:
            gather(j, final[j])
        else:
            x_copies[j].append((z, remote(j, final[j], place(z, j, xhi), device(2, 0, 0, 0))))

    def gather(j, src):
        up = remote(j, src, gathered(z, j), device(0, 0, 1, 0))
        down = remote(j, src, gathered(z, j), device(0, 0, -1, 0))
        spread(j, z, src)
        c_copies[j] = [up, down]

    def complete(j):
        x_copies[j][0][1].wait_recv()
        locals_[j][1].wait()
        gather(j, gathered(z, j))

    def forward(j):
        up, down = c_copies[j]
        up.wait_recv()
        part = place(below, j, xhi, 0)
        f_up = remote(j, part, part, device(0, 0, 1, 0))
        spread(j, below, gathered(below, j))
        down.wait_recv()
        part = place(above, j, xhi, 1)
        f_down = remote(j, part, part, device(0, 0, -1, 0))
        spread(j, above, gathered(above, j))
        c_copies[j] = [f_up, f_down]

    def forwarded(j):
        for cp in c_copies[j]:
            cp.wait_recv()
        spread(j, far, gathered(far, j))

    def crossed(j):
        for zz, cp in x_copies[j]:
            cp.wait_recv()
            part = place(zz, j, 1 - xhi)
            sides.append(remote(j, part, part, device(0, 0, 0, 1)))

    steps = {
        True: (pick_and_send, merge, forward, forwarded, crossed),
        False: (pick_and_send, merge, complete, forward, forwarded),
    }
    for j in range(AHEAD):
        compute(j)
        start_a(j)
    for t in range(NCH + max(AGES)):
        if t + AHEAD < NCH:
            compute(t + AHEAD)
        for stage in (0, 1, 2, 3, 4):
            j = t - AGES[stage]
            if 0 <= j < NCH:
                steps[CHUNKS[j][2]][stage](j)
                if stage == 0 and j + AHEAD < NCH:
                    start_a(j + AHEAD)
    for cp in sides:
        cp.wait_recv()
    for j in range(NCH):
        if CHUNKS[j][2]:
            locals_[j][1].wait()
    for cp in everything:
        cp.wait_send()
    for out in outs:
        out.wait()


def exchange(order, record):
    bf16 = jnp.bfloat16
    sizes = [(n, n // 2) for _, n, _ in CHUNKS]
    table = jnp.asarray(banded_table())
    scratch = [pltpu.SMEM(order.shape, order.dtype), pltpu.VMEM(table.shape, bf16)]
    scratch += [pltpu.VMEM(record.shape, bf16), pltpu.VMEM((8, PIECE, CH), bf16)]
    scratch += [pltpu.VMEM((8, n, CH), bf16) for n, _ in sizes]
    scratch += [pltpu.VMEM((ROUNDS, n, CH), bf16) for n, _ in sizes]
    scratch += [pltpu.VMEM((ROUNDS, 2, w, CH), bf16) for _, w in sizes]
    scratch += [pltpu.VMEM((ROUNDS, w, CH), bf16) for _, w in sizes]
    scratch += [
        pltpu.SemaphoreType.DMA((NCH, NSEM)),
        pltpu.SemaphoreType.DMA((NCH, NSEM)),
        pltpu.SemaphoreType.DMA((NCH, 2)),
        pltpu.SemaphoreType.DMA((2 * NCH + 2,)),
    ]
    return pl.pallas_call(
        exchange_kernel,
        out_shape=(
            jax.ShapeDtypeStruct((ROUNDS, 8, PIECE, CH), bf16),
            jax.ShapeDtypeStruct((8, PIECE, CH), bf16),
        ),
        in_specs=[
            pl.BlockSpec(memory_space=pltpu.HBM),
            pl.BlockSpec(memory_space=pltpu.HBM),
            pl.BlockSpec(memory_space=pltpu.HBM),
        ],
        out_specs=(pl.BlockSpec(memory_space=pl.ANY), pl.BlockSpec(memory_space=pl.ANY)),
        scratch_shapes=scratch,
        compiler_params=pltpu.CompilerParams(
            has_side_effects=True, vmem_limit_bytes=26 * 2**20
        ),
        name="exchange",
    )(*(pltpu.with_memory_space_constraint(v, pltpu.HBM) for v in (order, table, record)))


def cross_kernel(own_ref, other_ref, o_ref):
    piece = pl.program_id(0)
    own = own_ref[piece].reshape(WIN // STEPW, 4, STEPW, CH)
    for b in range(2):
        p = own[:, 2 * b].reshape(WIN, CH)
        q = own[:, 2 * b + 1].reshape(WIN, CH)
        pt, qt = p.T, q.T
        left = jnp.concatenate(
            [jnp.concatenate([pt, qt], axis=1), jnp.concatenate([qt, -pt], axis=1)], axis=0
        )
        for r in range(ROUNDS):
            other = other_ref[r, piece].reshape(WIN // STEPW, 4, STEPW, CH)
            right = jnp.concatenate(
                [other[:, 2 * b].reshape(WIN, CH), other[:, 2 * b + 1].reshape(WIN, CH)], axis=0
            )
            out = jnp.dot(left, right, preferred_element_type=jnp.float32)
            out = (out * (1.0 / math.sqrt(WIN))).astype(jnp.bfloat16)
            o_ref[r, 0, b] = out[:CH]
            o_ref[r, 1, b] = out[CH:]


def cross(s, g):
    return pl.pallas_call(
        cross_kernel,
        grid=(8,),
        out_shape=jax.ShapeDtypeStruct((ROUNDS, 2, NB, CH, CH), jnp.bfloat16),
        in_specs=[
            pl.BlockSpec(memory_space=pltpu.VMEM),
            pl.BlockSpec(memory_space=pltpu.VMEM),
        ],
        out_specs=pl.BlockSpec((ROUNDS, 2, 2, CH, CH), lambda f: (0, 0, f, 0, 0)),
        compiler_params=pltpu.CompilerParams(vmem_limit_bytes=12 * 2**20),
        name="cross",
    )(s, g)


def body(record, owner_order):
    g, s = exchange(owner_order, record)
    return cross(s, g)


def solution(mesh):
    placed = (P(None, ("blk", "grp")), P())
    return jax.shard_map(
        body,
        mesh=mesh,
        in_specs=placed,
        out_specs=P(None, None, None, ("blk", "grp"), None),
        check_vma=False,
    )
```
